32 devices in a mesh: groups: 2 (over x), tile: 16 (over z, y, core).
Axes of the slice: x: 2, y: 2, z: 4, core: 2. Of those that a mesh axis runs over, the one named last changes fastest.
Arguments:
- walkers: bfloat16 [32, 512, 256], P(('groups', 'tile')), parts along dimension 0, may hold values from -6 to 6
- green_factor: bfloat16 [32, 512, 256], P(('groups', 'tile')), parts along dimension 0, may hold values from -6 to 6
- trial: bfloat16 [512, 256], replicated, may hold values from -0.375 to 0.375
- chol: bfloat16 [496, 2048, 256], P('tile'), may hold values from -0.01171875 to 0.01171875
- pattern: int32 [256], replicated, may hold values from 0 to 1023, as said below
- owner_counts: int32 [16], replicated, may hold values from 1 to 31, as said below
- chol_group: int32 [2048], replicated, may hold values from 0 to 3
- group_weight: float32 [4], replicated, may hold values from 0.5 to 2
- aux: int32 [32, 2048], P('groups'), parts along dimension 0, may hold values from -524288 to 524287
Outputs:
- advanced: bfloat16 [32, 512, 256], P(('groups', 'tile')), parts along dimension 0
- log_weight: float32 [32], P(('groups', 'tile')), parts along dimension 0
The draws below stay inside these ranges and needn't reach their ends.
There are 2 independent parts, one for each index of `groups`. The reference program is written for one: setup_inputs(seed, part) draws one part's arguments, and reference() takes and returns one part's arrays. A program takes and returns all parts, laid end to end along the dimension named above; an argument that names none is the same for every part. Nothing has to cross between parts.
Inputs may be any that keep to these rules, and one draw needn't show every extreme that they name: `pattern`: values are distinct. Owners d and d + 8 together hold 32 tiles; slots of owner d past owner_counts[d] hold no tile.
All inputs are finite; a program needn't handle non-finite values.
Results may differ from the reference program's by a relative error of at most 0.009.
Values may be sent and summed in bfloat16 or wider, within the bound.
No kernel may reach another device: no remote copies, remote signals or barrier semaphores. Data moves between devices by JAX's collectives and lax.ppermute only.
A program may use at most 128 MiB of HBM per device.

```python
import math
import jax
import jax.numpy as jnp
from jax import lax

M = 512
NE = 256
NCHOL = 2048
NGRP = 4
NBLK = 32
BS2 = 256
NT = 256
CAP = 31
W = 16
N_TILE = 16


def draw_pattern(key, part):
    pair_count = NBLK * NBLK
    middle = jax.random.permutation(jax.random.fold_in(key, 11), pair_count - 2) + 1
    chosen = jnp.concatenate([jnp.array([0, pair_count - 1], jnp.int32), middle[:NT - 2].astype(jnp.int32)])
    shuffle = jax.random.permutation(jax.random.fold_in(key, 12), NT)
    return chosen[shuffle].astype(jnp.int32)


def draw_owner_counts(key, part):
    half_axis = N_TILE // 2
    per_device = NT // N_TILE
    first_half = jax.random.randint(jax.random.fold_in(key, 21), (half_axis,), 1, 2 * per_device, dtype=jnp.int32)
    heavy_slot = jax.random.randint(jax.random.fold_in(key, 22), (), 0, half_axis, dtype=jnp.int32)
    first_half = jnp.where(jnp.arange(half_axis, dtype=jnp.int32) == heavy_slot, 2 * per_device - 1, first_half)
    flipped = jax.random.randint(jax.random.fold_in(key, 23), (half_axis,), 0, 2, dtype=jnp.int32)
    lower = jnp.where(flipped == 1, 2 * per_device - first_half, first_half)
    return jnp.concatenate([lower, 2 * per_device - lower]).astype(jnp.int32)


def set_ends(entries, own_key, least, largest):
    spot = [jax.random.randint(jax.random.fold_in(own_key, axis), (), 0, length) for axis, length in enumerate(entries.shape)]
    longest = entries.shape.index(max(entries.shape))
    next_to = spot[:longest] + [(spot[longest] + 1) % entries.shape[longest]] + spot[longest + 1:]
    return entries.at[tuple(spot)].set(least).at[tuple(next_to)].set(largest)


def level_of(own_key, dims, pieces, smallest, largest):
    gain = 1.0
    for position, parts in pieces:
        draws = jax.random.uniform(jax.random.fold_in(jax.random.fold_in(own_key, 6), position), (parts,), jnp.float32, smallest / len(pieces), largest / len(pieces))
        gain = gain * jnp.repeat(jnp.exp(draws), dims[position] // parts).reshape((-1,) + (1,) * (len(dims) - 1 - position))
    return gain


def scatter_about(key, dims, deviation, reach, pieces=(), kind=jnp.bfloat16):
    values = deviation * jax.random.normal(key, dims, jnp.float32)
    if pieces:
        values = values * level_of(key, dims, pieces, -0.22, 0.18)
    return jnp.clip(values, -reach, reach).astype(kind)


def setup_inputs(seed: int = 0, part: int = 0) -> dict:
    key_list = jax.random.split(jax.random.key(seed), 10)
    own_keys = jax.random.split(jax.random.fold_in(key_list[9], part), 10)
    walkers = scatter_about(own_keys[0], (W, M, NE), 1.0, 6.0, ((0, 16),))
    green_factor = scatter_about(own_keys[1], (W, M, NE), 1.0, 6.0, ((0, 16),))
    trial = scatter_about(key_list[2], (M, NE), NE ** -0.5, 0.375)
    chol = scatter_about(key_list[3], (N_TILE * CAP, NCHOL, BS2), (NCHOL * M // 4) ** -0.5, 0.01171875, ((0, 16),))
    pattern = draw_pattern(jax.random.fold_in(key_list[9], 71), part)
    owner_counts = draw_owner_counts(jax.random.fold_in(key_list[9], 71), part)
    chol_group = set_ends(jax.random.randint(key_list[6], (NCHOL,), 0, NGRP), jax.random.fold_in(key_list[6], 1), 0, NGRP - 1).astype(jnp.int32)
    group_weight = jnp.clip(jnp.exp(jax.random.uniform(key_list[7], (NGRP,), jnp.float32, math.log(0.5), math.log(2.0))), 0.5, 2.0)
    aux = set_ends(jax.random.randint(own_keys[8], (W, NCHOL), -524288, 524288), jax.random.fold_in(own_keys[8], 1), -524288, 524287).astype(jnp.int32)
    return {"walkers": walkers, "green_factor": green_factor, "trial": trial, "chol": chol, "pattern": pattern, "owner_counts": owner_counts, "chol_group": chol_group, "group_weight": group_weight, "aux": aux}


def tile_slots(owner_counts):
    offsets = jnp.cumsum(owner_counts) - owner_counts
    tile_ids = jnp.arange(NT, dtype=jnp.int32)
    tile_ends = offsets + owner_counts
    owner_of = jnp.sum((tile_ids[:, None] >= tile_ends[None, :]).astype(jnp.int32), axis=1).astype(jnp.int32)
    return (owner_of * CAP + tile_ids - offsets[owner_of]).astype(jnp.int32)


def reference(walkers, green_factor, trial, chol, pattern, owner_counts, chol_group, group_weight, aux):
    block_side = M // NBLK
    row_blocks = (pattern // NBLK).astype(jnp.int32)
    col_blocks = (pattern % NBLK).astype(jnp.int32)
    chol_tiles = chol[tile_slots(owner_counts)]

    def green_tiles(factor_rows):
        green_full = jnp.dot(factor_rows, trial.T, preferred_element_type=jnp.float32).astype(jnp.bfloat16)
        blocks = green_full.reshape(NBLK, block_side, NBLK, block_side)
        return blocks[row_blocks, :, col_blocks, :].reshape(NT, block_side * block_side)

    green_all = lax.map(green_tiles, green_factor)
    force_bias = jnp.einsum("wte,tge->wg", green_all.astype(jnp.float32), chol_tiles.astype(jnp.float32))
    sampled = aux.astype(jnp.float32) * (1.0 / 262144.0)
    log_weight = jnp.sum(sampled * force_bias - 0.5 * force_bias * force_bias, axis=1)
    column_weight = group_weight[chol_group]
    fields = (column_weight[None, :] * (sampled - force_bias)).astype(jnp.bfloat16)
    potential = jnp.einsum("wg,tge->wte", fields.astype(jnp.float32), chol_tiles.astype(jnp.float32)).astype(jnp.bfloat16)

    def propagate(pair_args):
        walker, pot_tiles = pair_args
        tile_mats = pot_tiles.reshape(NT, block_side, block_side).astype(jnp.float32)
        taylor_term = walker
        running = walker.astype(jnp.float32)
        for degree in range(1, 5):
            gathered = taylor_term.reshape(NBLK, block_side, NE)[col_blocks].astype(jnp.float32)
            product = jnp.einsum("tpq,tqe->tpe", tile_mats, gathered)
            summed = jax.ops.segment_sum(product, row_blocks, num_segments=NBLK).reshape(M, NE)
            taylor_term = (summed / degree).astype(jnp.bfloat16)
            running = running + taylor_term.astype(jnp.float32)
        return running.astype(jnp.bfloat16)

    advanced = lax.map(propagate, (walkers, potential))
    return advanced, log_weight
```

```python
import functools
import math

import jax
import jax.numpy as jnp
from jax import lax
from jax.experimental import pallas as pl
from jax.experimental.pallas import tpu as pltpu
from jax.sharding import PartitionSpec as P

BF = jnp.bfloat16
F32 = jnp.float32
LANES = 128
VMEM_LIMIT = 60 * 1024 * 1024


def log2(n):
    bits = n.bit_length() - 1
    assert 1 << bits == n
    return bits


def iota(shape, axis):
    return lax.broadcasted_iota(jnp.int32, shape, axis)


def one_hot(equal):
    return jnp.where(equal, 1.0, 0.0).astype(BF)


def mm(a, b):
    return jnp.dot(a, b, preferred_element_type=F32)


def nt(a, b):
    return lax.dot_general(a, b, (((1,), (1,)), ((), ())), preferred_element_type=F32)


def swap_rows(outer, inner):
    n = outer * inner
    row, col = iota((n, n), 0), iota((n, n), 1)
    source = ((row & (outer - 1)) << log2(inner)) + (row >> log2(outer))
    return one_hot(source == col)


def regroup(x, outer, inner, chunk):
    take = swap_rows(chunk, inner)
    size = chunk * inner
    parts = [mm(take, x[i * size : (i + 1) * size]).astype(BF) for i in range(outer // chunk)]
    if len(parts) == 1:
        return parts[0]
    return jnp.concatenate(
        [part[b * chunk : (b + 1) * chunk] for b in range(inner) for part in parts], axis=0
    )


def ungroup(x, outer, inner, chunk):
    take = swap_rows(inner, chunk)
    parts = []
    for i in range(outer // chunk):
        rows = [x[b * outer + i * chunk : b * outer + (i + 1) * chunk] for b in range(inner)]
        piece = x if outer == chunk else jnp.concatenate(rows, axis=0)
        parts.append(mm(take, piece).astype(BF))
    return parts[0] if len(parts) == 1 else jnp.concatenate(parts, axis=0)


def slot_of_tile(counts_ref, tiles, owners, groups, half, cap):
    tile = iota((1, tiles), 1)
    owner = jnp.zeros((1, tiles), jnp.int32)
    first = jnp.zeros((1, tiles), jnp.int32)
    offset = jnp.int32(0)
    for d in range(owners):
        offset = offset + counts_ref[d]
        past = tile >= offset
        owner = jnp.where(past, d + 1, owner)
        first = jnp.where(past, offset, first)
    place = tile - first
    slot = owner * half + place
    for x in range(1, groups):
        start = min(x * half, cap - half)
        slot = jnp.where(place >= x * half, (x * owners + owner) * half + place - start, slot)
    return slot


def tile_columns(pattern_ref, tiles, nblk, side):
    pat = jnp.broadcast_to(pattern_ref[...].astype(F32), (LANES, tiles)).T.astype(jnp.int32)
    row_block = pat >> log2(nblk)
    col_block = pat & (nblk - 1)
    per = LANES // side
    return ((col_block >> log2(per)) << log2(nblk)) + row_block, col_block & (per - 1)


def green_kernel(
    counts_ref, pattern_ref, factor_ref, trial_ref, out_ref, *, owners, groups, half, cap, side
):
    orbitals = factor_ref.shape[0]
    nblk = orbitals // side
    tiles = pattern_ref.shape[1]
    wide = orbitals // LANES
    factor = mm(swap_rows(nblk, side), factor_ref[...]).astype(BF)
    green = nt(factor, trial_ref[...]).astype(BF)
    cut = jnp.concatenate(
        [
            jnp.concatenate(
                [
                    green[p * nblk : (p + 1) * nblk, k * LANES : (k + 1) * LANES]
                    for p in range(side)
                ],
                axis=1,
            )
            for k in range(wide)
        ],
        axis=0,
    )
    where_row, place = tile_columns(pattern_ref, tiles, nblk, side)
    lane = iota((tiles, LANES), 1)
    pick = one_hot(where_row == lane)
    inside = place == (lane >> log2(side))
    found = mm(pick, cut)
    kept = jnp.concatenate(
        [
            jnp.where(inside, found[:, p * LANES : (p + 1) * LANES], 0.0).astype(BF)
            for p in range(side)
        ],
        axis=1,
    )
    entries = side * side
    src = iota((side * LANES, entries), 0)
    dst = iota((side * LANES, entries), 1)
    fold = one_hot(((src >> log2(LANES)) << log2(side)) + (src & (side - 1)) == dst)
    values = mm(kept, fold).astype(BF)
    slot = slot_of_tile(counts_ref, tiles, owners, groups, half, cap)
    slots = out_ref.shape[0]
    out_ref[...] = mm(one_hot(iota((slots, tiles), 0) == slot), values).astype(BF)


def start_tiles(start_ref, chol_ref, held, sems, half):
    def begin(j, carry):
        pltpu.make_async_copy(chol_ref.at[start_ref[0] + j], held.at[j], sems.at[j]).start()
        return carry

    lax.fori_loop(0, half, begin, 0)


def wait_tile(chol_ref, held, sems, j):
    pltpu.make_async_copy(chol_ref.at[0], held.at[j], sems.at[j]).wait()


def bias_kernel(start_ref, green_ref, chol_ref, out_ref, held, rows, total, sems, *, walkers, half):
    start_tiles(start_ref, chol_ref, held, sems, half)
    chunk = min(walkers, max(1, 512 // half))
    rows[...] = regroup(green_ref[...], walkers, half, chunk)
    total[...] = jnp.zeros_like(total)

    def step(j, carry):
        wait_tile(chol_ref, held, sems, j)
        left = rows[pl.ds(pl.multiple_of(j * walkers, walkers), walkers), :]
        total[...] += nt(left, held[j])
        return carry

    lax.fori_loop(0, half, step, 0)
    vectors = total.shape[1]
    lanes = vectors // LANES
    stacked = jnp.concatenate(
        [total[:, i * LANES : (i + 1) * LANES].astype(BF) for i in range(lanes)], axis=0
    )
    out_ref[...] = ungroup(stacked, walkers, lanes, min(walkers, max(1, 512 // lanes)))


def field_kernel(
    index_ref, weight_ref, partial_ref, aux_ref, group_ref, fields_ref, logw_ref, *, devices
):
    lanes = group_ref.shape[0]
    bias = jnp.zeros((lanes, LANES), F32)
    for i in range(devices):
        bias = bias + partial_ref[i].astype(F32)
    draws = aux_ref[pl.ds(index_ref[0], 1), :]
    draws = jnp.concatenate(
        [draws[:, i * LANES : (i + 1) * LANES] for i in range(lanes)], axis=0
    )
    sampled = draws.astype(F32) * (1.0 / 262144.0)
    weight = jnp.zeros((lanes, LANES), F32)
    for k in range(weight_ref.shape[0]):
        weight = jnp.where(group_ref[...] == k, weight_ref[k], weight)
    fields = (weight * (sampled - bias)).astype(BF)
    for i in range(devices):
        fields_ref[i] = fields
    logw_ref[0] = jnp.sum(sampled * bias - 0.5 * bias * bias)


def potential_kernel(start_ref, fields_ref, chol_ref, out_ref, held, left, rows, sems, *, walkers, half):
    start_tiles(start_ref, chol_ref, held, sems, half)
    vectors = left.shape[1]
    lanes = vectors // LANES
    stacked = regroup(fields_ref[...], walkers, lanes, min(walkers, max(1, 512 // lanes)))
    for i in range(lanes):
        left[:, i * LANES : (i + 1) * LANES] = stacked[i * walkers : (i + 1) * walkers]

    def step(j, carry):
        wait_tile(chol_ref, held, sems, j)
        rows[pl.ds(pl.multiple_of(j * walkers, walkers), walkers), :] = mm(
            left[...], held[j]
        ).astype(BF)
        return carry

    lax.fori_loop(0, half, step, 0)
    out_ref[...] = ungroup(rows[...], walkers, half, min(walkers, max(1, 512 // half)))


def advance_kernel(
    counts_ref, pattern_ref, tiles_ref, walker_ref, out_ref, *, owners, groups, half, cap, side
):
    orbitals = walker_ref.shape[0]
    nblk = orbitals // side
    tiles = pattern_ref.shape[1]
    wide = orbitals // LANES
    entries = side * side
    slots = tiles_ref.shape[0]
    slot = slot_of_tile(counts_ref, tiles, owners, groups, half, cap)
    place_in = one_hot(iota((slots, tiles), 0) == slot)
    values = lax.dot_general(
        place_in, tiles_ref[...], (((0,), (0,)), ((), ())), preferred_element_type=F32
    ).astype(BF)
    src = iota((entries, side * LANES), 0)
    dst = iota((entries, side * LANES), 1)
    spread = one_hot(((dst >> log2(LANES)) << log2(side)) + (dst & (side - 1)) == src)
    where_row, place = tile_columns(pattern_ref, tiles, nblk, side)
    lane = iota((tiles, LANES), 1)
    inside = place == (lane >> log2(side))
    repeated = mm(values, spread)
    kept = jnp.concatenate(
        [
            jnp.where(inside, repeated[:, p * LANES : (p + 1) * LANES], 0.0).astype(BF)
            for p in range(side)
        ],
        axis=1,
    )
    pick = one_hot(where_row == lane)
    cut = lax.dot_general(
        pick, kept, (((0,), (0,)), ((), ())), preferred_element_type=F32
    ).astype(BF)
    mixed = jnp.concatenate(
        [
            jnp.concatenate(
                [
                    cut[k * nblk : (k + 1) * nblk, p * LANES : (p + 1) * LANES]
                    for k in range(wide)
                ],
                axis=1,
            )
            for p in range(side)
        ],
        axis=0,
    )
    potential = mm(swap_rows(side, nblk), mixed).astype(BF)
    term = walker_ref[...]
    running = term.astype(F32)
    for degree in range(1, 5):
        term = (mm(potential, term) / degree).astype(BF)
        running = running + term.astype(F32)
    out_ref[...] = running.astype(BF)


def per_device(
    walkers, green_factor, trial, chol, pattern, owner_counts, chol_group, group_weight, aux, *, groups, owners
):
    devices = groups * owners
    walk_dev, orbitals, electrons = walkers.shape
    assert walk_dev == 1
    cap, vectors, entries = chol.shape
    side = math.isqrt(entries)
    lanes = vectors // LANES
    half = -(-cap // groups)
    tiles = pattern.shape[0]
    both = ("groups", "tile")
    my_group = lax.axis_index("groups")
    start = jnp.minimum(my_group * half, cap - half).astype(jnp.int32).reshape(1)
    my_index = lax.axis_index("tile").astype(jnp.int32).reshape(1)
    pattern_row = pattern.reshape(1, tiles)

    smem = pl.BlockSpec(memory_space=pltpu.SMEM)
    vmem = pl.BlockSpec(memory_space=pltpu.VMEM)
    hbm = pl.BlockSpec(memory_space=pl.ANY)
    params = pltpu.CompilerParams(vmem_limit_bytes=VMEM_LIMIT)
    sizes = dict(owners=owners, groups=groups, half=half, cap=cap, side=side)

    outgoing = pl.pallas_call(
        functools.partial(green_kernel, **sizes),
        out_shape=jax.ShapeDtypeStruct((devices * half, entries), BF),
        in_specs=[smem, vmem, vmem, vmem],
        out_specs=vmem,
        compiler_params=params,
        name="green",
    )(owner_counts, pattern_row, green_factor[0], trial)
    arrived = lax.all_to_all(
        outgoing.reshape(devices, half, entries), both, split_axis=0, concat_axis=0
    )
    partial_bias = pl.pallas_call(
        functools.partial(bias_kernel, walkers=devices, half=half),
        out_shape=jax.ShapeDtypeStruct((devices * lanes, LANES), BF),
        in_specs=[smem, vmem, hbm],
        out_specs=vmem,
        scratch_shapes=[
            pltpu.VMEM((half, vectors, entries), BF),
            pltpu.VMEM((half * devices, entries), BF),
            pltpu.VMEM((devices, vectors), F32),
            pltpu.SemaphoreType.DMA((half,)),
        ],
        compiler_params=params,
        name="bias",
    )(start, arrived.reshape(devices * half, entries), chol)
    partial_bias = lax.all_to_all(
        partial_bias.reshape(devices, lanes, LANES), both, split_axis=0, concat_axis=0
    )
    fields, log_weight = pl.pallas_call(
        functools.partial(field_kernel, devices=devices),
        out_shape=(
            jax.ShapeDtypeStruct((devices, lanes, LANES), BF),
            jax.ShapeDtypeStruct((1,), F32),
        ),
        in_specs=[smem, smem, vmem, vmem, vmem],
        out_specs=(vmem, smem),
        compiler_params=params,
        name="fields",
    )(my_index, group_weight, partial_bias, aux, chol_group.reshape(lanes, LANES))
    fields = lax.all_to_all(fields, both, split_axis=0, concat_axis=0)
    potential = pl.pallas_call(
        functools.partial(potential_kernel, walkers=devices, half=half),
        out_shape=jax.ShapeDtypeStruct((devices * half, entries), BF),
        in_specs=[smem, vmem, hbm],
        out_specs=vmem,
        scratch_shapes=[
            pltpu.VMEM((half, vectors, entries), BF),
            pltpu.VMEM((devices, vectors), BF),
            pltpu.VMEM((half * devices, entries), BF),
            pltpu.SemaphoreType.DMA((half,)),
        ],
        compiler_params=params,
        name="potential",
    )(start, fields.reshape(devices * lanes, LANES), chol)
    returned = lax.all_to_all(
        potential.reshape(devices, half, entries), both, split_axis=0, concat_axis=0
    )
    advanced = pl.pallas_call(
        functools.partial(advance_kernel, **sizes),
        out_shape=jax.ShapeDtypeStruct((orbitals, electrons), BF),
        in_specs=[smem, vmem, vmem, vmem],
        out_specs=vmem,
        compiler_params=params,
        name="advance",
    )(owner_counts, pattern_row, returned.reshape(devices * half, entries), walkers[0])
    return advanced[None], log_weight


def solution(mesh):
    return jax.shard_map(
        functools.partial(
            per_device, groups=mesh.shape["groups"], owners=mesh.shape["tile"]
        ),
        mesh=mesh,
        in_specs=(
            P(("groups", "tile"), None, None),
            P(("groups", "tile"), None, None),
            P(),
            P("tile", None, None),
            P(),
            P(),
            P(),
            P(),
            P("groups", None),
        ),
        out_specs=(P(("groups", "tile"), None, None), P(("groups", "tile"))),
        check_vma=False,
    )
```

```python
import functools
import math

import jax
import jax.numpy as jnp
from jax import lax
from jax.experimental import pallas as pl
from jax.experimental.pallas import tpu as pltpu
from jax.sharding import PartitionSpec as P

BF = jnp.bfloat16
F32 = jnp.float32
LANES = 128
VMEM_LIMIT = 8 * 1024 * 1024


def log2(n):
    bits = n.bit_length() - 1
    assert 1 << bits == n
    return bits


def iota(shape, axis):
    return lax.broadcasted_iota(jnp.int32, shape, axis)


def one_hot(equal):
    return jnp.where(equal, 1.0, 0.0).astype(BF)


def mm(a, b):
    return jnp.dot(a, b, preferred_element_type=F32)


def nt(a, b):
    return lax.dot_general(a, b, (((1,), (1,)), ((), ())), preferred_element_type=F32)


def slot_of_tile(counts_ref, tiles, owners, groups, half, cap):
    tile = iota((1, tiles), 1)
    owner = jnp.zeros((1, tiles), jnp.int32)
    first = jnp.zeros((1, tiles), jnp.int32)
    offset = jnp.int32(0)
    for d in range(owners):
        offset = offset + counts_ref[d]
        past = tile >= offset
        owner = jnp.where(past, d + 1, owner)
        first = jnp.where(past, offset, first)
    place = tile - first
    slot = owner * half + place
    for x in range(1, groups):
        start = min(x * half, cap - half)
        slot = jnp.where(place >= x * half, (x * owners + owner) * half + place - start, slot)
    return slot


def tile_columns(pattern_ref, tiles, nblk, side):
    pat = jnp.broadcast_to(pattern_ref[...].astype(F32), (LANES, tiles)).T.astype(jnp.int32)
    row_block = pat >> log2(nblk)
    col_block = pat & (nblk - 1)
    per = LANES // side
    return ((col_block >> log2(per)) << log2(nblk)) + row_block, col_block & (per - 1)


def green_kernel(
    counts_ref, pattern_ref, factor_ref, trial_ref, out_ref, wide_ref, *, owners, groups, half, cap, side
):
    orbitals = factor_ref.shape[0]
    nblk = orbitals // side
    tiles = pattern_ref.shape[1]
    wide = orbitals // LANES
    assert wide * nblk == LANES
    green = nt(factor_ref[...], trial_ref[...])
    for k in range(wide):
        wide_ref[k] = green[:, k * LANES : (k + 1) * LANES]
    cut = jnp.concatenate(
        [
            jnp.concatenate(
                [wide_ref[k, pl.ds(p, nblk, stride=side), :] for p in range(side)], axis=1
            ).astype(BF)
            for k in range(wide)
        ],
        axis=0,
    )
    where_row, place = tile_columns(pattern_ref, tiles, nblk, side)
    lane = iota((tiles, LANES), 1)
    pick = one_hot(where_row == lane)
    inside = place == (lane >> log2(side))
    found = mm(pick, cut)
    kept = jnp.concatenate(
        [
            jnp.where(inside, found[:, p * LANES : (p + 1) * LANES], 0.0).astype(BF)
            for p in range(side)
        ],
        axis=1,
    )
    entries = side * side
    src = iota((side * LANES, entries), 0)
    dst = iota((side * LANES, entries), 1)
    fold = one_hot(((src >> log2(LANES)) << log2(side)) + (src & (side - 1)) == dst)
    values = mm(kept, fold).astype(BF)
    slot = slot_of_tile(counts_ref, tiles, owners, groups, half, cap)
    slots = out_ref.shape[0]
    out_ref[...] = mm(one_hot(iota((slots, tiles), 0) == slot), values).astype(BF)


def first_slot(half, cap):
    return jnp.minimum(lax.axis_index("groups") * half, cap - half)


def block_sizes(vectors):
    if vectors % 1024:
        return [vectors]
    return [512] * (vectors // 512 - 1) + [256, 256]


def bias_kernel(green_ref, chol_ref, out_ref, tall, left, back, held, sems, *, walkers, half):
    entries = green_ref.shape[1]
    vectors = held.shape[1]
    lanes = vectors // LANES
    narrow = entries // LANES
    first = first_slot(half, chol_ref.shape[0])
    blocks = block_sizes(vectors)
    starts = [sum(blocks[:s]) for s in range(len(blocks))]
    part = half // 4 if half % 4 == 0 else 1
    copies = [
        [
            pltpu.make_async_copy(
                chol_ref.at[pl.ds(first + j, part), pl.ds(at, size), :],
                held.at[pl.ds(j, part), pl.ds(at, size), :],
                sems.at[s, j // part],
            )
            for j in range(0, half, part)
        ]
        for s, (at, size) in enumerate(zip(starts, blocks))
    ]
    for group in copies:
        for copy in group:
            copy.start()
    for k in range(narrow):
        tall[k] = green_ref[:, k * LANES : (k + 1) * LANES].astype(F32)
    for j in range(half):
        for k in range(narrow):
            at = j * entries + k * LANES
            left[:, at : at + LANES] = tall[k, pl.ds(j, walkers, stride=half), :].astype(BF)
    for at, size, group in zip(starts, blocks, copies):
        for copy in group:
            copy.wait()
        right = jnp.concatenate([held[j, at : at + size, :] for j in range(half)], axis=1)
        total = nt(left[...], right)
        for i in range(size // LANES):
            back[pl.ds(at // LANES + i, walkers, stride=lanes), :] = total[
                :, i * LANES : (i + 1) * LANES
            ]
    out_ref[...] = back[...].astype(BF)


def field_kernel(
    weight_ref, partial_ref, aux_ref, group_ref, fields_ref, logw_ref, *, devices
):
    lanes = group_ref.shape[0]
    bias = jnp.zeros((lanes, LANES), F32)
    for i in range(devices):
        bias = bias + partial_ref[i].astype(F32)
    draws = aux_ref[pl.ds(lax.axis_index("tile"), 1), :]
    draws = jnp.concatenate(
        [draws[:, i * LANES : (i + 1) * LANES] for i in range(lanes)], axis=0
    )
    sampled = draws.astype(F32) * (1.0 / 262144.0)
    weight = jnp.zeros((lanes, LANES), F32)
    for k in range(weight_ref.shape[0]):
        weight = jnp.where(group_ref[...] == k, weight_ref[k], weight)
    fields = (weight * (sampled - bias)).astype(BF)
    for i in range(devices):
        fields_ref[i] = fields
    logw_ref[0] = jnp.sum(sampled * bias - 0.5 * bias * bias)


def potential_kernel(fields_ref, chol_ref, out_ref, tall, left, back, held, sems, *, walkers, half):
    entries = held.shape[2]
    lanes = left.shape[1] // LANES
    narrow = entries // LANES
    first = first_slot(half, chol_ref.shape[0])
    copies = [
        pltpu.make_async_copy(chol_ref.at[first + j], held.at[j], sems.at[j]) for j in range(half)
    ]
    for copy in copies:
        copy.start()
    tall[...] = fields_ref[...].astype(F32)
    for i in range(lanes):
        left[:, i * LANES : (i + 1) * LANES] = tall[pl.ds(i, walkers, stride=lanes), :].astype(BF)
    for j in range(half):
        copies[j].wait()
        tile = mm(left[...], held[j])
        for k in range(narrow):
            back[k, pl.ds(j, walkers, stride=half), :] = tile[:, k * LANES : (k + 1) * LANES]
    for k in range(narrow):
        out_ref[:, k * LANES : (k + 1) * LANES] = back[k].astype(BF)


def advance_kernel(
    counts_ref, pattern_ref, tiles_ref, walker_ref, out_ref, wide_ref, *, owners, groups, half, cap, side
):
    orbitals = walker_ref.shape[0]
    nblk = orbitals // side
    tiles = pattern_ref.shape[1]
    wide = orbitals // LANES
    entries = side * side
    slots = tiles_ref.shape[0]
    slot = slot_of_tile(counts_ref, tiles, owners, groups, half, cap)
    place_in = one_hot(iota((slots, tiles), 0) == slot)
    values = lax.dot_general(
        place_in, tiles_ref[...], (((0,), (0,)), ((), ())), preferred_element_type=F32
    ).astype(BF)
    src = iota((entries, side * LANES), 0)
    dst = iota((entries, side * LANES), 1)
    spread = one_hot(((dst >> log2(LANES)) << log2(side)) + (dst & (side - 1)) == src)
    where_row, place = tile_columns(pattern_ref, tiles, nblk, side)
    lane = iota((tiles, LANES), 1)
    inside = place == (lane >> log2(side))
    repeated = mm(values, spread)
    kept = jnp.concatenate(
        [
            jnp.where(inside, repeated[:, p * LANES : (p + 1) * LANES], 0.0).astype(BF)
            for p in range(side)
        ],
        axis=1,
    )
    pick = one_hot(where_row == lane)
    cut = lax.dot_general(
        pick, kept, (((0,), (0,)), ((), ())), preferred_element_type=F32
    )
    for k in range(wide):
        for p in range(side):
            wide_ref[k, pl.ds(p, nblk, stride=side), :] = cut[
                k * nblk : (k + 1) * nblk, p * LANES : (p + 1) * LANES
            ]
    potential = jnp.concatenate([wide_ref[k].astype(BF) for k in range(wide)], axis=1)
    term = walker_ref[...]
    running = term.astype(F32)
    for degree in range(1, 5):
        term = (mm(potential, term) / degree).astype(BF)
        running = running + term.astype(F32)
    out_ref[...] = running.astype(BF)


def per_device(
    walkers, green_factor, trial, chol, pattern, owner_counts, chol_group, group_weight, aux, *, groups, owners
):
    devices = groups * owners
    walk_dev, orbitals, electrons = walkers.shape
    assert walk_dev == 1
    cap, vectors, entries = chol.shape
    side = math.isqrt(entries)
    lanes = vectors // LANES
    half = -(-cap // groups)
    tiles = pattern.shape[0]
    both = ("groups", "tile")
    pattern_row = pattern.reshape(1, tiles)

    smem = pl.BlockSpec(memory_space=pltpu.SMEM)
    vmem = pl.BlockSpec(memory_space=pltpu.VMEM)
    params = pltpu.CompilerParams(vmem_limit_bytes=VMEM_LIMIT)
    hbm = pl.BlockSpec(memory_space=pl.ANY)
    streaming = pltpu.CompilerParams(
        vmem_limit_bytes=VMEM_LIMIT + 2 * half * vectors * entries
    )
    large = pltpu.CompilerParams(vmem_limit_bytes=60 * 1024 * 1024)
    sizes = dict(owners=owners, groups=groups, half=half, cap=cap, side=side)
    tile_bytes = half * vectors * entries * 2
    flops = 2 * devices * half * vectors * entries
    wide_scratch = pltpu.VMEM((orbitals // LANES, orbitals, LANES), F32)

    outgoing = pl.pallas_call(
        functools.partial(green_kernel, **sizes),
        out_shape=jax.ShapeDtypeStruct((devices * half, entries), BF),
        in_specs=[smem, vmem, vmem, vmem],
        out_specs=vmem,
        scratch_shapes=[wide_scratch],
        compiler_params=large,
        name="green",
    )(owner_counts, pattern_row, green_factor[0], trial)
    arrived = lax.all_to_all(
        outgoing.reshape(devices, half, entries), both, split_axis=0, concat_axis=0
    )
    partial_bias = pl.pallas_call(
        functools.partial(bias_kernel, walkers=devices, half=half),
        out_shape=jax.ShapeDtypeStruct((devices * lanes, LANES), BF),
        in_specs=[vmem, hbm],
        out_specs=vmem,
        scratch_shapes=[
            pltpu.VMEM((entries // LANES, half * devices, LANES), F32),
            pltpu.VMEM((devices, half * entries), BF),
            pltpu.VMEM((devices * lanes, LANES), F32),
            pltpu.VMEM((half, vectors, entries), BF),
            pltpu.SemaphoreType.DMA((len(block_sizes(vectors)), half)),
        ],
        compiler_params=streaming,
        cost_estimate=pl.CostEstimate(
            flops=flops, transcendentals=0, bytes_accessed=tile_bytes
        ),
        name="bias",
    )(arrived.reshape(devices * half, entries), chol)
    partial_bias = lax.all_to_all(
        partial_bias.reshape(devices, lanes, LANES), both, split_axis=0, concat_axis=0
    )
    fields, log_weight = pl.pallas_call(
        functools.partial(field_kernel, devices=devices),
        out_shape=(
            jax.ShapeDtypeStruct((devices, lanes, LANES), BF),
            jax.ShapeDtypeStruct((1,), F32),
        ),
        in_specs=[smem, vmem, vmem, vmem],
        out_specs=(vmem, smem),
        compiler_params=params,
        name="fields",
    )(group_weight, partial_bias, aux, chol_group.reshape(lanes, LANES))
    fields = lax.all_to_all(fields, both, split_axis=0, concat_axis=0)
    potential = pl.pallas_call(
        functools.partial(potential_kernel, walkers=devices, half=half),
        out_shape=jax.ShapeDtypeStruct((devices * half, entries), BF),
        in_specs=[vmem, hbm],
        out_specs=vmem,
        scratch_shapes=[
            pltpu.VMEM((devices * lanes, LANES), F32),
            pltpu.VMEM((devices, vectors), BF),
            pltpu.VMEM((entries // LANES, half * devices, LANES), F32),
            pltpu.VMEM((half, vectors, entries), BF),
            pltpu.SemaphoreType.DMA((half,)),
        ],
        compiler_params=streaming,
        cost_estimate=pl.CostEstimate(
            flops=flops, transcendentals=0, bytes_accessed=tile_bytes
        ),
        name="potential",
    )(fields.reshape(devices * lanes, LANES), chol)
    returned = lax.all_to_all(
        potential.reshape(devices, half, entries), both, split_axis=0, concat_axis=0
    )
    advanced = pl.pallas_call(
        functools.partial(advance_kernel, **sizes),
        out_shape=jax.ShapeDtypeStruct((orbitals, electrons), BF),
        in_specs=[smem, vmem, vmem, vmem],
        out_specs=vmem,
        scratch_shapes=[wide_scratch],
        compiler_params=params,
        name="advance",
    )(owner_counts, pattern_row, returned.reshape(devices * half, entries), walkers[0])
    return advanced[None], log_weight


def solution(mesh):
    return jax.shard_map(
        functools.partial(
            per_device, groups=mesh.shape["groups"], owners=mesh.shape["tile"]
        ),
        mesh=mesh,
        in_specs=(
            P(("groups", "tile"), None, None),
            P(("groups", "tile"), None, None),
            P(),
            P("tile", None, None),
            P(),
            P(),
            P(),
            P(),
            P("groups", None),
        ),
        out_specs=(P(("groups", "tile"), None, None), P(("groups", "tile"))),
        check_vma=False,
    )
```

```python
import functools
import math

import jax
import jax.numpy as jnp
from jax import lax
from jax.experimental import pallas as pl
from jax.experimental.pallas import tpu as pltpu
from jax.sharding import PartitionSpec as P

BF = jnp.bfloat16
F32 = jnp.float32
LANES = 128
VMEM_LIMIT = 8 * 1024 * 1024


def log2(n):
    bits = n.bit_length() - 1
    assert 1 << bits == n
    return bits


def iota(shape, axis):
    return lax.broadcasted_iota(jnp.int32, shape, axis)


def one_hot(equal):
    return jnp.where(equal, 1.0, 0.0).astype(BF)


def mm(a, b):
    return jnp.dot(a, b, preferred_element_type=F32)


def nt(a, b):
    return lax.dot_general(a, b, (((1,), (1,)), ((), ())), preferred_element_type=F32)


def slot_of_tile(counts_ref, tiles, owners, groups, half, cap):
    tile = iota((1, tiles), 1)
    owner = jnp.zeros((1, tiles), jnp.int32)
    first = jnp.zeros((1, tiles), jnp.int32)
    offset = jnp.int32(0)
    for d in range(owners):
        offset = offset + counts_ref[d]
        past = tile >= offset
        owner = jnp.where(past, d + 1, owner)
        first = jnp.where(past, offset, first)
    place = tile - first
    slot = owner * half + place
    for x in range(1, groups):
        start = min(x * half, cap - half)
        slot = jnp.where(place >= x * half, (x * owners + owner) * half + place - start, slot)
    return slot


def row_of(pat, nblk, side):
    row_block = pat >> log2(nblk)
    col_block = pat & (nblk - 1)
    per = LANES // side
    return ((col_block >> log2(per)) << log2(nblk)) + row_block, col_block & (per - 1)


def tile_columns(pattern_ref, tiles, nblk, side):
    pat = jnp.broadcast_to(pattern_ref[...].astype(F32), (LANES, tiles)).T.astype(jnp.int32)
    return row_of(pat, nblk, side)


def green_kernel(
    counts_ref, pattern_ref, factor_ref, trial_ref, out_ref, wide_ref, *, owners, groups, half, cap, side
):
    orbitals = factor_ref.shape[0]
    nblk = orbitals // side
    tiles = pattern_ref.shape[1]
    wide = orbitals // LANES
    assert wide * nblk == LANES
    green = nt(factor_ref[...], trial_ref[...])
    for k in range(wide):
        wide_ref[k] = green[:, k * LANES : (k + 1) * LANES]
    cut = jnp.concatenate(
        [
            jnp.concatenate(
                [wide_ref[k, pl.ds(p, nblk, stride=side), :] for p in range(side)], axis=1
            ).astype(BF)
            for k in range(wide)
        ],
        axis=0,
    )
    where_row, place = tile_columns(pattern_ref, tiles, nblk, side)
    lane = iota((tiles, LANES), 1)
    pick = one_hot(where_row == lane)
    inside = place == (lane >> log2(side))
    found = mm(pick, cut)
    kept = jnp.concatenate(
        [
            jnp.where(inside, found[:, p * LANES : (p + 1) * LANES], 0.0).astype(BF)
            for p in range(side)
        ],
        axis=1,
    )
    entries = side * side
    src = iota((side * LANES, entries), 0)
    dst = iota((side * LANES, entries), 1)
    fold = one_hot(((src >> log2(LANES)) << log2(side)) + (src & (side - 1)) == dst)
    values = mm(kept, fold).astype(BF)
    slot = slot_of_tile(counts_ref, tiles, owners, groups, half, cap)
    slots = out_ref.shape[0]
    out_ref[...] = mm(one_hot(iota((slots, tiles), 0) == slot), values).astype(BF)


def first_slot(half, cap):
    return jnp.minimum(lax.axis_index("groups") * half, cap - half)


def bias_kernel(green_ref, chol_ref, out_ref, tall, left, back, held, sems, *, walkers, half, block):
    entries = green_ref.shape[1]
    vectors = held.shape[1]
    lanes = vectors // LANES
    narrow = entries // LANES
    steps = vectors // block
    first = first_slot(half, chol_ref.shape[0])

    def fetch(s):
        rows = pl.ds(s * block if isinstance(s, int) else pl.multiple_of(s * block, block), block)
        return pltpu.make_async_copy(
            chol_ref.at[pl.ds(first, half), rows, :], held.at[:, rows, :], sems.at[s]
        )

    for s in range(steps):
        fetch(s).start()
    for k in range(narrow):
        tall[k] = green_ref[:, k * LANES : (k + 1) * LANES].astype(F32)
    for j in range(half):
        for k in range(narrow):
            at = j * entries + k * LANES
            left[:, at : at + LANES] = tall[k, pl.ds(j, walkers, stride=half), :].astype(BF)

    def step(s, carry):
        fetch(s).wait()
        rows = pl.ds(pl.multiple_of(s * block, block), block)
        right = jnp.concatenate([held[j, rows, :] for j in range(half)], axis=1)
        total = nt(left[...], right)
        for i in range(block // LANES):
            place = s * (block // LANES) + i
            back[pl.ds(place, walkers, stride=lanes), :] = total[:, i * LANES : (i + 1) * LANES]
        return carry

    lax.fori_loop(0, steps, step, 0)
    out_ref[...] = back[...].astype(BF)


def field_kernel(
    weight_ref, partial_ref, aux_ref, group_ref, fields_ref, logw_ref, *, devices
):
    lanes = group_ref.shape[0]
    bias = jnp.zeros((lanes, LANES), F32)
    for i in range(devices):
        bias = bias + partial_ref[i].astype(F32)
    draws = aux_ref[pl.ds(lax.axis_index("tile"), 1), :]
    draws = jnp.concatenate(
        [draws[:, i * LANES : (i + 1) * LANES] for i in range(lanes)], axis=0
    )
    sampled = draws.astype(F32) * (1.0 / 262144.0)
    weight = jnp.zeros((lanes, LANES), F32)
    for k in range(weight_ref.shape[0]):
        weight = jnp.where(group_ref[...] == k, weight_ref[k], weight)
    fields = (weight * (sampled - bias)).astype(BF)
    for i in range(devices):
        fields_ref[i] = fields
    logw_ref[0] = jnp.sum(sampled * bias - 0.5 * bias * bias)


def potential_kernel(fields_ref, chol_ref, out_ref, tall, left, back, held, sems, *, walkers, half):
    entries = held.shape[2]
    lanes = left.shape[1] // LANES
    narrow = entries // LANES
    first = first_slot(half, chol_ref.shape[0])

    def fetch(j):
        return pltpu.make_async_copy(chol_ref.at[first + j], held.at[j], sems.at[j])

    def begin(j, carry):
        fetch(j).start()
        return carry

    lax.fori_loop(0, half, begin, 0)
    tall[...] = fields_ref[...].astype(F32)
    for i in range(lanes):
        left[:, i * LANES : (i + 1) * LANES] = tall[pl.ds(i, walkers, stride=lanes), :].astype(BF)

    def step(j, carry):
        fetch(j).wait()
        tile = mm(left[...], held[j])
        for k in range(narrow):
            back[k, pl.ds(j, walkers, stride=half), :] = tile[:, k * LANES : (k + 1) * LANES]
        return carry

    lax.fori_loop(0, half, step, 0)
    for k in range(narrow):
        out_ref[:, k * LANES : (k + 1) * LANES] = back[k].astype(BF)


def prepare_kernel(
    counts_ref, pattern_ref, after_ref, place_ref, spread_ref, pick_ref, inside_ref, *, owners, groups, half, cap, side, nblk
):
    del after_ref
    tiles, slots = place_ref.shape
    slot = slot_of_tile(counts_ref, tiles, owners, groups, half, cap)
    slot = jnp.broadcast_to(slot.astype(F32), (LANES, tiles)).T.astype(jnp.int32)
    lane = iota((tiles, LANES), 1)
    for k in range(slots // LANES):
        place_ref[:, k * LANES : (k + 1) * LANES] = one_hot(slot == lane + k * LANES)
    src = iota(spread_ref.shape, 0)
    dst = iota(spread_ref.shape, 1)
    spread_ref[...] = one_hot(((dst >> log2(LANES)) << log2(side)) + (dst & (side - 1)) == src)
    where_row, _ = row_of(pattern_ref[...], nblk, side)
    pick_ref[...] = one_hot(iota((LANES, tiles), 0) == where_row)
    _, place = tile_columns(pattern_ref, tiles, nblk, side)
    inside_ref[...] = jnp.where(place == (lane >> log2(side)), 1.0, 0.0)


def advance_kernel(
    tiles_ref, place_ref, spread_ref, pick_ref, inside_ref, walker_ref, out_ref, wide_ref, *, side
):
    orbitals = walker_ref.shape[0]
    nblk = orbitals // side
    wide = orbitals // LANES
    values = mm(place_ref[...], tiles_ref[...]).astype(BF)
    repeated = mm(values, spread_ref[...])
    inside = inside_ref[...]
    kept = jnp.concatenate(
        [(repeated[:, p * LANES : (p + 1) * LANES] * inside).astype(BF) for p in range(side)],
        axis=1,
    )
    cut = mm(pick_ref[...], kept)
    for k in range(wide):
        for p in range(side):
            wide_ref[k, pl.ds(p, nblk, stride=side), :] = cut[
                k * nblk : (k + 1) * nblk, p * LANES : (p + 1) * LANES
            ]
    potential = jnp.concatenate([wide_ref[k].astype(BF) for k in range(wide)], axis=1)
    term = walker_ref[...]
    running = term.astype(F32)
    for degree in range(1, 5):
        term = (mm(potential, term) / degree).astype(BF)
        running = running + term.astype(F32)
    out_ref[...] = running.astype(BF)


def per_device(
    walkers, green_factor, trial, chol, pattern, owner_counts, chol_group, group_weight, aux, *, groups, owners
):
    devices = groups * owners
    walk_dev, orbitals, electrons = walkers.shape
    assert walk_dev == 1
    cap, vectors, entries = chol.shape
    side = math.isqrt(entries)
    lanes = vectors // LANES
    half = -(-cap // groups)
    tiles = pattern.shape[0]
    both = ("groups", "tile")
    pattern_row = pattern.reshape(1, tiles)

    smem = pl.BlockSpec(memory_space=pltpu.SMEM)
    vmem = pl.BlockSpec(memory_space=pltpu.VMEM)
    params = pltpu.CompilerParams(vmem_limit_bytes=VMEM_LIMIT)
    hbm = pl.BlockSpec(memory_space=pl.ANY)
    streaming = pltpu.CompilerParams(
        vmem_limit_bytes=VMEM_LIMIT + 2 * half * vectors * entries
    )
    large = pltpu.CompilerParams(vmem_limit_bytes=60 * 1024 * 1024)
    sizes = dict(owners=owners, groups=groups, half=half, cap=cap, side=side)
    block = min(256, vectors)
    tile_bytes = half * vectors * entries * 2
    flops = 2 * devices * half * vectors * entries
    wide_scratch = pltpu.VMEM((orbitals // LANES, orbitals, LANES), F32)

    outgoing = pl.pallas_call(
        functools.partial(green_kernel, **sizes),
        out_shape=jax.ShapeDtypeStruct((devices * half, entries), BF),
        in_specs=[smem, vmem, vmem, vmem],
        out_specs=vmem,
        scratch_shapes=[wide_scratch],
        compiler_params=large,
        name="green",
    )(owner_counts, pattern_row, green_factor[0], trial)
    arrived = lax.all_to_all(
        outgoing.reshape(devices, half, entries), both, split_axis=0, concat_axis=0
    )
    partial_bias = pl.pallas_call(
        functools.partial(bias_kernel, walkers=devices, half=half, block=block),
        out_shape=jax.ShapeDtypeStruct((devices * lanes, LANES), BF),
        in_specs=[vmem, hbm],
        out_specs=vmem,
        scratch_shapes=[
            pltpu.VMEM((entries // LANES, half * devices, LANES), F32),
            pltpu.VMEM((devices, half * entries), BF),
            pltpu.VMEM((devices * lanes, LANES), F32),
            pltpu.VMEM((half, vectors, entries), BF),
            pltpu.SemaphoreType.DMA((vectors // block,)),
        ],
        compiler_params=streaming,
        cost_estimate=pl.CostEstimate(
            flops=flops, transcendentals=0, bytes_accessed=tile_bytes
        ),
        name="bias",
    )(arrived.reshape(devices * half, entries), chol)
    partial_bias = lax.all_to_all(
        partial_bias.reshape(devices, lanes, LANES), both, split_axis=0, concat_axis=0
    )
    fields, log_weight = pl.pallas_call(
        functools.partial(field_kernel, devices=devices),
        out_shape=(
            jax.ShapeDtypeStruct((devices, lanes, LANES), BF),
            jax.ShapeDtypeStruct((1,), F32),
        ),
        in_specs=[smem, vmem, vmem, vmem],
        out_specs=(vmem, smem),
        compiler_params=params,
        name="fields",
    )(group_weight, partial_bias, aux, chol_group.reshape(lanes, LANES))
    fields = lax.all_to_all(fields, both, split_axis=0, concat_axis=0)
    potential = pl.pallas_call(
        functools.partial(potential_kernel, walkers=devices, half=half),
        out_shape=jax.ShapeDtypeStruct((devices * half, entries), BF),
        in_specs=[vmem, hbm],
        out_specs=vmem,
        scratch_shapes=[
            pltpu.VMEM((devices * lanes, LANES), F32),
            pltpu.VMEM((devices, vectors), BF),
            pltpu.VMEM((entries // LANES, half * devices, LANES), F32),
            pltpu.VMEM((half, vectors, entries), BF),
            pltpu.SemaphoreType.DMA((half,)),
        ],
        compiler_params=streaming,
        cost_estimate=pl.CostEstimate(
            flops=flops, transcendentals=0, bytes_accessed=tile_bytes
        ),
        name="potential",
    )(fields.reshape(devices * lanes, LANES), chol)
    returned = lax.all_to_all(
        potential.reshape(devices, half, entries), both, split_axis=0, concat_axis=0
    )
    spread_width = side * LANES
    prepared = pl.pallas_call(
        functools.partial(prepare_kernel, nblk=orbitals // side, **sizes),
        out_shape=(
            jax.ShapeDtypeStruct((tiles, devices * half), BF),
            jax.ShapeDtypeStruct((entries, spread_width), BF),
            jax.ShapeDtypeStruct((LANES, tiles), BF),
            jax.ShapeDtypeStruct((tiles, LANES), F32),
        ),
        in_specs=[smem, vmem, hbm],
        out_specs=(vmem, vmem, vmem, vmem),
        compiler_params=params,
        cost_estimate=pl.CostEstimate(
            flops=10 * entries * spread_width, transcendentals=0, bytes_accessed=1 << 22
        ),
        name="prepare",
    )(owner_counts, pattern_row, potential)
    advanced = pl.pallas_call(
        functools.partial(advance_kernel, side=side),
        out_shape=jax.ShapeDtypeStruct((orbitals, electrons), BF),
        in_specs=[vmem] * 6,
        out_specs=vmem,
        scratch_shapes=[wide_scratch],
        compiler_params=params,
        name="advance",
    )(returned.reshape(devices * half, entries), *prepared, walkers[0])
    return advanced[None], log_weight


def solution(mesh):
    return jax.shard_map(
        functools.partial(
            per_device, groups=mesh.shape["groups"], owners=mesh.shape["tile"]
        ),
        mesh=mesh,
        in_specs=(
            P(("groups", "tile"), None, None),
            P(("groups", "tile"), None, None),
            P(),
            P("tile", None, None),
            P(),
            P(),
            P(),
            P(),
            P("groups", None),
        ),
        out_specs=(P(("groups", "tile"), None, None), P(("groups", "tile"))),
        check_vma=False,
    )
```

```python
import functools
import math

import jax
import jax.numpy as jnp
from jax import lax
from jax.experimental import pallas as pl
from jax.experimental.pallas import tpu as pltpu
from jax.sharding import PartitionSpec as P

BF = jnp.bfloat16
F32 = jnp.float32
LANES = 128
VMEM_LIMIT = 8 * 1024 * 1024


def log2(n):
    bits = n.bit_length() - 1
    assert 1 << bits == n
    return bits


def iota(shape, axis):
    return lax.broadcasted_iota(jnp.int32, shape, axis)


def one_hot(equal):
    return jnp.where(equal, 1.0, 0.0).astype(BF)


def mm(a, b):
    return jnp.dot(a, b, preferred_element_type=F32)


def nt(a, b):
    return lax.dot_general(a, b, (((1,), (1,)), ((), ())), preferred_element_type=F32)


def slot_of_tile(counts_ref, tiles, owners, groups, half, cap):
    tile = iota((1, tiles), 1)
    owner = jnp.zeros((1, tiles), jnp.int32)
    first = jnp.zeros((1, tiles), jnp.int32)
    offset = jnp.int32(0)
    for d in range(owners):
        offset = offset + counts_ref[d]
        past = tile >= offset
        owner = jnp.where(past, d + 1, owner)
        first = jnp.where(past, offset, first)
    place = tile - first
    slot = owner * half + place
    for x in range(1, groups):
        start = min(x * half, cap - half)
        slot = jnp.where(place >= x * half, (x * owners + owner) * half + place - start, slot)
    return slot


def row_of(pat, nblk, side):
    row_block = pat >> log2(nblk)
    col_block = pat & (nblk - 1)
    per = LANES // side
    return ((col_block >> log2(per)) << log2(nblk)) + row_block, col_block & (per - 1)


def tile_columns(pattern_ref, tiles, nblk, side):
    pat = jnp.broadcast_to(pattern_ref[...].astype(F32), (LANES, tiles)).T.astype(jnp.int32)
    return row_of(pat, nblk, side)


def green_kernel(
    counts_hbm, pattern_hbm, factor_hbm, trial_hbm, out_ref,
    counts_ref, pattern_ref, factor_ref, trial_ref, wide_ref, fold_ref, slot_ref, sems,
    *, owners, groups, half, cap, side,
):
    copies = [
        pltpu.make_async_copy(source, held, sems.at[i])
        for i, (source, held) in enumerate(
            [
                (counts_hbm, counts_ref),
                (pattern_hbm, pattern_ref),
                (factor_hbm, factor_ref),
                (trial_hbm, trial_ref),
            ]
        )
    ]
    for copy in copies:
        copy.start()
    orbitals = factor_ref.shape[0]
    nblk = orbitals // side
    tiles = pattern_ref.shape[1]
    slots = out_ref.shape[0]
    wide = orbitals // LANES
    assert wide * nblk == LANES
    src = iota(fold_ref.shape, 0)
    dst = iota(fold_ref.shape, 1)
    fold_ref[...] = one_hot(((src >> log2(LANES)) << log2(side)) + (src & (side - 1)) == dst)
    copies[0].wait()
    copies[1].wait()
    where_row, place = tile_columns(pattern_ref, tiles, nblk, side)
    lane = iota((tiles, LANES), 1)
    pick = one_hot(where_row == lane)
    inside = place == (lane >> log2(side))
    slot = slot_of_tile(counts_ref, tiles, owners, groups, half, cap)
    slot_ref[...] = one_hot(iota((slots, tiles), 0) == slot)
    copies[2].wait()
    copies[3].wait()
    green = nt(factor_ref[...], trial_ref[...])
    for k in range(wide):
        wide_ref[k] = green[:, k * LANES : (k + 1) * LANES]
    cut = jnp.concatenate(
        [
            jnp.concatenate(
                [wide_ref[k, pl.ds(p, nblk, stride=side), :] for p in range(side)], axis=1
            ).astype(BF)
            for k in range(wide)
        ],
        axis=0,
    )
    found = mm(pick, cut)
    kept = jnp.concatenate(
        [
            jnp.where(inside, found[:, p * LANES : (p + 1) * LANES], 0.0).astype(BF)
            for p in range(side)
        ],
        axis=1,
    )
    values = mm(kept, fold_ref[...]).astype(BF)
    out_ref[...] = mm(slot_ref[...], values).astype(BF)


def in_place(x):
    return pltpu.with_memory_space_constraint(x, pltpu.HBM)


def first_slot(half, cap):
    return jnp.minimum(lax.axis_index("groups") * half, cap - half)


def bias_kernel(green_ref, chol_ref, out_ref, tall, left, back, held, sems, *, walkers, half, block):
    entries = green_ref.shape[1]
    vectors = held.shape[1]
    lanes = vectors // LANES
    narrow = entries // LANES
    steps = vectors // block
    first = first_slot(half, chol_ref.shape[0])

    def fetch(s):
        rows = pl.ds(s * block if isinstance(s, int) else pl.multiple_of(s * block, block), block)
        return pltpu.make_async_copy(
            chol_ref.at[pl.ds(first, half), rows, :], held.at[:, rows, :], sems.at[s]
        )

    for s in range(steps):
        fetch(s).start()
    for k in range(narrow):
        tall[k] = green_ref[:, k * LANES : (k + 1) * LANES].astype(F32)
    for j in range(half):
        for k in range(narrow):
            at = j * entries + k * LANES
            left[:, at : at + LANES] = tall[k, pl.ds(j, walkers, stride=half), :].astype(BF)

    def step(s, carry):
        fetch(s).wait()
        rows = pl.ds(pl.multiple_of(s * block, block), block)
        right = jnp.concatenate([held[j, rows, :] for j in range(half)], axis=1)
        total = nt(left[...], right)
        for i in range(block // LANES):
            place = s * (block // LANES) + i
            back[pl.ds(place, walkers, stride=lanes), :] = total[:, i * LANES : (i + 1) * LANES]
        return carry

    lax.fori_loop(0, steps, step, 0)
    out_ref[...] = back[...].astype(BF)


def field_kernel(
    weight_ref, partial_ref, aux_ref, group_ref, fields_ref, logw_ref, *, devices
):
    lanes = group_ref.shape[0]
    bias = jnp.zeros((lanes, LANES), F32)
    for i in range(devices):
        bias = bias + partial_ref[i].astype(F32)
    draws = aux_ref[pl.ds(lax.axis_index("tile"), 1), :]
    draws = jnp.concatenate(
        [draws[:, i * LANES : (i + 1) * LANES] for i in range(lanes)], axis=0
    )
    sampled = draws.astype(F32) * (1.0 / 262144.0)
    weight = jnp.zeros((lanes, LANES), F32)
    for k in range(weight_ref.shape[0]):
        weight = jnp.where(group_ref[...] == k, weight_ref[k], weight)
    fields = (weight * (sampled - bias)).astype(BF)
    for i in range(devices):
        fields_ref[i] = fields
    logw_ref[0] = jnp.sum(sampled * bias - 0.5 * bias * bias)


def prepare(
    counts_ref, pattern_ref, place_ref, spread_ref, pick_ref, inside_ref, *, owners, groups, half, cap, side, nblk
):
    tiles, slots = place_ref.shape
    lane = iota((tiles, LANES), 1)
    slot = slot_of_tile(counts_ref, tiles, owners, groups, half, cap)
    slot = jnp.broadcast_to(slot.astype(F32), (LANES, tiles)).T.astype(jnp.int32)
    for k in range(slots // LANES):
        place_ref[:, k * LANES : (k + 1) * LANES] = one_hot(slot == lane + k * LANES)
    src = iota(spread_ref.shape, 0)
    dst = iota(spread_ref.shape, 1)
    spread_ref[...] = one_hot(((dst >> log2(LANES)) << log2(side)) + (dst & (side - 1)) == src)
    where_row, _ = row_of(pattern_ref[...], nblk, side)
    pick_ref[...] = one_hot(iota((LANES, tiles), 0) == where_row)
    _, place = tile_columns(pattern_ref, tiles, nblk, side)
    inside_ref[...] = jnp.where(place == (lane >> log2(side)), 1.0, 0.0)


def potential_kernel(
    counts_ref, pattern_ref, fields_ref, chol_ref,
    out_ref, place_ref, spread_ref, pick_ref, inside_ref,
    tall, left, back, held, sems, *, walkers, half, **sizes,
):
    entries = held.shape[2]
    lanes = left.shape[1] // LANES
    narrow = entries // LANES
    first = first_slot(half, chol_ref.shape[0])

    def fetch(j):
        return pltpu.make_async_copy(chol_ref.at[first + j], held.at[j], sems.at[j])

    def begin(j, carry):
        fetch(j).start()
        return carry

    lax.fori_loop(0, half, begin, 0)
    prepare(
        counts_ref, pattern_ref, place_ref, spread_ref, pick_ref, inside_ref, half=half, **sizes
    )
    tall[...] = fields_ref[...].astype(F32)
    for i in range(lanes):
        left[:, i * LANES : (i + 1) * LANES] = tall[pl.ds(i, walkers, stride=lanes), :].astype(BF)

    def step(j, carry):
        fetch(j).wait()
        tile = mm(left[...], held[j])
        for k in range(narrow):
            back[k, pl.ds(j, walkers, stride=half), :] = tile[:, k * LANES : (k + 1) * LANES]
        return carry

    lax.fori_loop(0, half, step, 0)
    for k in range(narrow):
        out_ref[:, k * LANES : (k + 1) * LANES] = back[k].astype(BF)


def advance_kernel(
    tiles_ref, place_ref, spread_ref, pick_ref, inside_ref, walker_ref, out_ref, wide_ref, *, side
):
    orbitals = walker_ref.shape[0]
    nblk = orbitals // side
    wide = orbitals // LANES
    values = mm(place_ref[...], tiles_ref[...]).astype(BF)
    repeated = mm(values, spread_ref[...])
    inside = inside_ref[...]
    kept = jnp.concatenate(
        [(repeated[:, p * LANES : (p + 1) * LANES] * inside).astype(BF) for p in range(side)],
        axis=1,
    )
    cut = mm(pick_ref[...], kept)
    for k in range(wide):
        for p in range(side):
            wide_ref[k, pl.ds(p, nblk, stride=side), :] = cut[
                k * nblk : (k + 1) * nblk, p * LANES : (p + 1) * LANES
            ]
    potential = jnp.concatenate([wide_ref[k].astype(BF) for k in range(wide)], axis=1)
    term = walker_ref[...]
    running = term.astype(F32)
    for degree in range(1, 5):
        term = (mm(potential, term) / degree).astype(BF)
        running = running + term.astype(F32)
    out_ref[...] = running.astype(BF)


def per_device(
    walkers, green_factor, trial, chol, pattern, owner_counts, chol_group, group_weight, aux, *, groups, owners
):
    devices = groups * owners
    walk_dev, orbitals, electrons = walkers.shape
    assert walk_dev == 1
    cap, vectors, entries = chol.shape
    side = math.isqrt(entries)
    lanes = vectors // LANES
    half = -(-cap // groups)
    tiles = pattern.shape[0]
    both = ("groups", "tile")
    pattern_row = pattern.reshape(1, tiles)

    smem = pl.BlockSpec(memory_space=pltpu.SMEM)
    vmem = pl.BlockSpec(memory_space=pltpu.VMEM)
    params = pltpu.CompilerParams(vmem_limit_bytes=VMEM_LIMIT)
    hbm = pl.BlockSpec(memory_space=pl.ANY)
    in_hbm = pl.BlockSpec(memory_space=pltpu.HBM)
    streaming = pltpu.CompilerParams(
        vmem_limit_bytes=VMEM_LIMIT + 2 * half * vectors * entries
    )
    sizes = dict(owners=owners, groups=groups, half=half, cap=cap, side=side)
    block = min(256, vectors)
    tile_bytes = half * vectors * entries * 2
    flops = 2 * devices * half * vectors * entries
    wide_scratch = pltpu.VMEM((orbitals // LANES, orbitals, LANES), F32)

    outgoing = pl.pallas_call(
        functools.partial(green_kernel, **sizes),
        out_shape=jax.ShapeDtypeStruct((devices * half, entries), BF),
        in_specs=[in_hbm] * 4,
        out_specs=vmem,
        scratch_shapes=[
            pltpu.SMEM(owner_counts.shape, jnp.int32),
            pltpu.VMEM((1, tiles), jnp.int32),
            pltpu.VMEM((orbitals, electrons), BF),
            pltpu.VMEM((orbitals, electrons), BF),
            wide_scratch,
            pltpu.VMEM((side * LANES, entries), BF),
            pltpu.VMEM((devices * half, tiles), BF),
            pltpu.SemaphoreType.DMA((4,)),
        ],
        compiler_params=params,
        name="green",
    )(*(in_place(x) for x in (owner_counts, pattern_row, green_factor[0], trial)))
    arrived = lax.all_to_all(
        outgoing.reshape(devices, half, entries), both, split_axis=0, concat_axis=0
    )
    partial_bias = pl.pallas_call(
        functools.partial(bias_kernel, walkers=devices, half=half, block=block),
        out_shape=jax.ShapeDtypeStruct((devices * lanes, LANES), BF),
        in_specs=[vmem, hbm],
        out_specs=vmem,
        scratch_shapes=[
            pltpu.VMEM((entries // LANES, half * devices, LANES), F32),
            pltpu.VMEM((devices, half * entries), BF),
            pltpu.VMEM((devices * lanes, LANES), F32),
            pltpu.VMEM((half, vectors, entries), BF),
            pltpu.SemaphoreType.DMA((vectors // block,)),
        ],
        compiler_params=streaming,
        cost_estimate=pl.CostEstimate(
            flops=flops, transcendentals=0, bytes_accessed=tile_bytes
        ),
        name="bias",
    )(arrived.reshape(devices * half, entries), chol)
    partial_bias = lax.all_to_all(
        partial_bias.reshape(devices, lanes, LANES), both, split_axis=0, concat_axis=0
    )
    fields, log_weight = pl.pallas_call(
        functools.partial(field_kernel, devices=devices),
        out_shape=(
            jax.ShapeDtypeStruct((devices, lanes, LANES), BF),
            jax.ShapeDtypeStruct((1,), F32),
        ),
        in_specs=[smem, vmem, vmem, vmem],
        out_specs=(vmem, smem),
        compiler_params=params,
        name="fields",
    )(group_weight, partial_bias, aux, chol_group.reshape(lanes, LANES))
    fields = lax.all_to_all(fields, both, split_axis=0, concat_axis=0)
    spread_width = side * LANES
    potential, *prepared = pl.pallas_call(
        functools.partial(
            potential_kernel, walkers=devices, nblk=orbitals // side, **sizes
        ),
        out_shape=(
            jax.ShapeDtypeStruct((devices * half, entries), BF),
            jax.ShapeDtypeStruct((tiles, devices * half), BF),
            jax.ShapeDtypeStruct((entries, spread_width), BF),
            jax.ShapeDtypeStruct((LANES, tiles), BF),
            jax.ShapeDtypeStruct((tiles, LANES), F32),
        ),
        in_specs=[smem, vmem, vmem, hbm],
        out_specs=(vmem,) * 5,
        scratch_shapes=[
            pltpu.VMEM((devices * lanes, LANES), F32),
            pltpu.VMEM((devices, vectors), BF),
            pltpu.VMEM((entries // LANES, half * devices, LANES), F32),
            pltpu.VMEM((half, vectors, entries), BF),
            pltpu.SemaphoreType.DMA((half,)),
        ],
        compiler_params=streaming,
        cost_estimate=pl.CostEstimate(
            flops=flops, transcendentals=0, bytes_accessed=tile_bytes
        ),
        name="potential",
    )(owner_counts, pattern_row, fields.reshape(devices * lanes, LANES), chol)
    returned = lax.all_to_all(
        potential.reshape(devices, half, entries), both, split_axis=0, concat_axis=0
    )
    advanced = pl.pallas_call(
        functools.partial(advance_kernel, side=side),
        out_shape=jax.ShapeDtypeStruct((orbitals, electrons), BF),
        in_specs=[vmem] * 6,
        out_specs=vmem,
        scratch_shapes=[wide_scratch],
        compiler_params=params,
        name="advance",
    )(returned.reshape(devices * half, entries), *prepared, walkers[0])
    return advanced[None], log_weight


def solution(mesh):
    return jax.shard_map(
        functools.partial(
            per_device, groups=mesh.shape["groups"], owners=mesh.shape["tile"]
        ),
        mesh=mesh,
        in_specs=(
            P(("groups", "tile"), None, None),
            P(("groups", "tile"), None, None),
            P(),
            P("tile", None, None),
            P(),
            P(),
            P(),
            P(),
            P("groups", None),
        ),
        out_specs=(P(("groups", "tile"), None, None), P(("groups", "tile"))),
        check_vma=False,
    )
```

```python
import functools
import math

import jax
import jax.numpy as jnp
from jax import lax
from jax.experimental import pallas as pl
from jax.experimental.pallas import tpu as pltpu
from jax.sharding import PartitionSpec as P

BF = jnp.bfloat16
F32 = jnp.float32
LANES = 128
VMEM_LIMIT = 8 * 1024 * 1024


def log2(n):
    bits = n.bit_length() - 1
    assert 1 << bits == n
    return bits


def iota(shape, axis):
    return lax.broadcasted_iota(jnp.int32, shape, axis)


def one_hot(equal):
    return jnp.where(equal, 1.0, 0.0).astype(BF)


def mm(a, b):
    return jnp.dot(a, b, preferred_element_type=F32)


def nt(a, b):
    return lax.dot_general(a, b, (((1,), (1,)), ((), ())), preferred_element_type=F32)


def slot_of_tile(counts_ref, tiles, owners, groups, half, cap):
    tile = iota((1, tiles), 1)
    owner = jnp.zeros((1, tiles), jnp.int32)
    first = jnp.zeros((1, tiles), jnp.int32)
    offset = jnp.int32(0)
    for d in range(owners):
        offset = offset + counts_ref[d]
        past = tile >= offset
        owner = jnp.where(past, d + 1, owner)
        first = jnp.where(past, offset, first)
    place = tile - first
    slot = owner * half + place
    for x in range(1, groups):
        start = min(x * half, cap - half)
        slot = jnp.where(place >= x * half, (x * owners + owner) * half + place - start, slot)
    return slot


def row_of(pat, nblk, side):
    row_block = pat >> log2(nblk)
    col_block = pat & (nblk - 1)
    per = LANES // side
    return ((col_block >> log2(per)) << log2(nblk)) + row_block, col_block & (per - 1)


def tile_columns(pattern_ref, tiles, nblk, side):
    pat = jnp.broadcast_to(pattern_ref[...].astype(F32), (LANES, tiles)).T.astype(jnp.int32)
    return row_of(pat, nblk, side)


def green_kernel(
    counts_hbm, pattern_hbm, factor_hbm, trial_hbm, out_ref,
    counts_ref, pattern_ref, factor_ref, trial_ref, wide_ref, fold_ref, slot_ref, sems,
    *, owners, groups, half, cap, side,
):
    copies = [
        pltpu.make_async_copy(source, held, sems.at[i])
        for i, (source, held) in enumerate(
            [
                (counts_hbm, counts_ref),
                (pattern_hbm, pattern_ref),
                (factor_hbm, factor_ref),
                (trial_hbm, trial_ref),
            ]
        )
    ]
    for copy in copies:
        copy.start()
    orbitals = factor_ref.shape[0]
    nblk = orbitals // side
    tiles = pattern_ref.shape[1]
    slots = out_ref.shape[0]
    wide = orbitals // LANES
    assert wide * nblk == LANES
    src = iota(fold_ref.shape, 0)
    dst = iota(fold_ref.shape, 1)
    fold_ref[...] = one_hot(((src >> log2(LANES)) << log2(side)) + (src & (side - 1)) == dst)
    copies[0].wait()
    copies[1].wait()
    where_row, place = tile_columns(pattern_ref, tiles, nblk, side)
    lane = iota((tiles, LANES), 1)
    pick = one_hot(where_row == lane)
    inside = place == (lane >> log2(side))
    slot = slot_of_tile(counts_ref, tiles, owners, groups, half, cap)
    slot_ref[...] = one_hot(iota((slots, tiles), 0) == slot)
    copies[2].wait()
    copies[3].wait()
    green = nt(factor_ref[...], trial_ref[...])
    for k in range(wide):
        wide_ref[k] = green[:, k * LANES : (k + 1) * LANES]
    cut = jnp.concatenate(
        [
            jnp.concatenate(
                [wide_ref[k, pl.ds(p, nblk, stride=side), :] for p in range(side)], axis=1
            ).astype(BF)
            for k in range(wide)
        ],
        axis=0,
    )
    found = mm(pick, cut)
    kept = jnp.concatenate(
        [
            jnp.where(inside, found[:, p * LANES : (p + 1) * LANES], 0.0).astype(BF)
            for p in range(side)
        ],
        axis=1,
    )
    values = mm(kept, fold_ref[...]).astype(BF)
    out_ref[...] = mm(slot_ref[...], values).astype(BF)


def in_place(x):
    return pltpu.with_memory_space_constraint(x, pltpu.HBM)


def first_slot(half, cap):
    return jnp.minimum(lax.axis_index("groups") * half, cap - half)


def draw_row(aux_ref, group_ref, weight_ref, sampled_ref, scale_ref):
    lanes = group_ref.shape[0]
    draws = aux_ref[pl.ds(lax.axis_index("tile"), 1), :]
    for i in range(lanes):
        sampled_ref[i : i + 1, :] = draws[:, i * LANES : (i + 1) * LANES].astype(F32) * (
            1.0 / 262144.0
        )
    scale = jnp.zeros(group_ref.shape, F32)
    for k in range(weight_ref.shape[0]):
        scale = jnp.where(group_ref[...] == k, weight_ref[k], scale)
    scale_ref[...] = scale


def bias_kernel(
    green_ref, chol_ref, aux_hbm, group_hbm, weight_hbm,
    out_ref, sampled_ref, scale_ref,
    tall, left, back, held, aux_ref, group_ref, weight_ref, side_sems, sems,
    *, walkers, half, block,
):
    entries = green_ref.shape[1]
    vectors = held.shape[1]
    lanes = vectors // LANES
    narrow = entries // LANES
    steps = vectors // block
    first = first_slot(half, chol_ref.shape[0])

    def fetch(s):
        rows = pl.ds(s * block if isinstance(s, int) else pl.multiple_of(s * block, block), block)
        return pltpu.make_async_copy(
            chol_ref.at[pl.ds(first, half), rows, :], held.at[:, rows, :], sems.at[s]
        )

    others = [
        pltpu.make_async_copy(source, dest, side_sems.at[i])
        for i, (source, dest) in enumerate(
            [(aux_hbm, aux_ref), (group_hbm, group_ref), (weight_hbm, weight_ref)]
        )
    ]
    for copy in others:
        copy.start()
    for s in range(steps):
        fetch(s).start()
    for k in range(narrow):
        tall[k] = green_ref[:, k * LANES : (k + 1) * LANES].astype(F32)
    for j in range(half):
        for k in range(narrow):
            at = j * entries + k * LANES
            left[:, at : at + LANES] = tall[k, pl.ds(j, walkers, stride=half), :].astype(BF)
    for copy in others:
        copy.wait()
    draw_row(aux_ref, group_ref, weight_ref, sampled_ref, scale_ref)

    def step(s, carry):
        fetch(s).wait()
        rows = pl.ds(pl.multiple_of(s * block, block), block)
        right = jnp.concatenate([held[j, rows, :] for j in range(half)], axis=1)
        total = nt(left[...], right)
        for i in range(block // LANES):
            place = s * (block // LANES) + i
            back[pl.ds(place, walkers, stride=lanes), :] = total[:, i * LANES : (i + 1) * LANES]
        return carry

    lax.fori_loop(0, steps, step, 0)
    out_ref[...] = back[...].astype(BF)


def field_kernel(partial_ref, sampled_ref, scale_ref, fields_ref, summand_ref, *, devices):
    bias = partial_ref[0].astype(F32)
    for i in range(1, devices):
        bias = bias + partial_ref[i].astype(F32)
    sampled = sampled_ref[...]
    fields = (scale_ref[...] * (sampled - bias)).astype(BF)
    for i in range(devices):
        fields_ref[i] = fields
    summand_ref[...] = sampled * bias - 0.5 * bias * bias


def prepare(
    counts_ref, pattern_ref, place_ref, spread_ref, pick_ref, inside_ref, *, owners, groups, half, cap, side, nblk
):
    tiles, slots = place_ref.shape
    lane = iota((tiles, LANES), 1)
    slot = slot_of_tile(counts_ref, tiles, owners, groups, half, cap)
    slot = jnp.broadcast_to(slot.astype(F32), (LANES, tiles)).T.astype(jnp.int32)
    for k in range(slots // LANES):
        place_ref[:, k * LANES : (k + 1) * LANES] = one_hot(slot == lane + k * LANES)
    src = iota(spread_ref.shape, 0)
    dst = iota(spread_ref.shape, 1)
    spread_ref[...] = one_hot(((dst >> log2(LANES)) << log2(side)) + (dst & (side - 1)) == src)
    where_row, _ = row_of(pattern_ref[...], nblk, side)
    pick_ref[...] = one_hot(iota((LANES, tiles), 0) == where_row)
    _, place = tile_columns(pattern_ref, tiles, nblk, side)
    inside_ref[...] = jnp.where(place == (lane >> log2(side)), 1.0, 0.0)


def potential_kernel(
    counts_hbm, pattern_ref, fields_ref, chol_ref,
    out_ref, place_ref, spread_ref, pick_ref, inside_ref,
    tall, left, back, held, counts_ref, counts_sem, sems, *, walkers, half, **sizes,
):
    entries = held.shape[2]
    lanes = left.shape[1] // LANES
    narrow = entries // LANES
    first = first_slot(half, chol_ref.shape[0])

    def fetch(j):
        return pltpu.make_async_copy(chol_ref.at[first + j], held.at[j], sems.at[j])

    def begin(j, carry):
        fetch(j).start()
        return carry

    counts = pltpu.make_async_copy(counts_hbm, counts_ref, counts_sem)
    counts.start()
    lax.fori_loop(0, half, begin, 0)
    counts.wait()
    prepare(
        counts_ref, pattern_ref, place_ref, spread_ref, pick_ref, inside_ref, half=half, **sizes
    )
    tall[...] = fields_ref[...].astype(F32)
    for i in range(lanes):
        left[:, i * LANES : (i + 1) * LANES] = tall[pl.ds(i, walkers, stride=lanes), :].astype(BF)

    def step(j, carry):
        fetch(j).wait()
        tile = mm(left[...], held[j])
        for k in range(narrow):
            back[k, pl.ds(j, walkers, stride=half), :] = tile[:, k * LANES : (k + 1) * LANES]
        return carry

    lax.fori_loop(0, half, step, 0)
    for k in range(narrow):
        out_ref[:, k * LANES : (k + 1) * LANES] = back[k].astype(BF)


def advance_kernel(
    tiles_ref, place_ref, spread_ref, pick_ref, inside_ref, walker_ref, summand_ref,
    out_ref, logw_ref, wide_ref, *, side,
):
    logw_ref[0] = jnp.sum(summand_ref[...])
    orbitals = walker_ref.shape[0]
    nblk = orbitals // side
    wide = orbitals // LANES
    values = mm(place_ref[...], tiles_ref[...]).astype(BF)
    repeated = mm(values, spread_ref[...])
    inside = inside_ref[...]
    kept = jnp.concatenate(
        [(repeated[:, p * LANES : (p + 1) * LANES] * inside).astype(BF) for p in range(side)],
        axis=1,
    )
    cut = mm(pick_ref[...], kept)
    for k in range(wide):
        for p in range(side):
            wide_ref[k, pl.ds(p, nblk, stride=side), :] = cut[
                k * nblk : (k + 1) * nblk, p * LANES : (p + 1) * LANES
            ]
    potential = jnp.concatenate([wide_ref[k].astype(BF) for k in range(wide)], axis=1)
    term = walker_ref[...]
    running = term.astype(F32)
    for degree in range(1, 5):
        term = (mm(potential, term) / degree).astype(BF)
        running = running + term.astype(F32)
    out_ref[...] = running.astype(BF)


def per_device(
    walkers, green_factor, trial, chol, pattern, owner_counts, chol_group, group_weight, aux, *, groups, owners
):
    devices = groups * owners
    walk_dev, orbitals, electrons = walkers.shape
    assert walk_dev == 1
    cap, vectors, entries = chol.shape
    side = math.isqrt(entries)
    lanes = vectors // LANES
    half = -(-cap // groups)
    tiles = pattern.shape[0]
    both = ("groups", "tile")
    pattern_row = pattern.reshape(1, tiles)

    smem = pl.BlockSpec(memory_space=pltpu.SMEM)
    vmem = pl.BlockSpec(memory_space=pltpu.VMEM)
    params = pltpu.CompilerParams(vmem_limit_bytes=VMEM_LIMIT)
    hbm = pl.BlockSpec(memory_space=pl.ANY)
    in_hbm = pl.BlockSpec(memory_space=pltpu.HBM)
    streaming = pltpu.CompilerParams(
        vmem_limit_bytes=VMEM_LIMIT + 2 * half * vectors * entries
    )
    sizes = dict(owners=owners, groups=groups, half=half, cap=cap, side=side)
    block = min(256, vectors)
    tile_bytes = half * vectors * entries * 2
    flops = 2 * devices * half * vectors * entries
    wide_scratch = pltpu.VMEM((orbitals // LANES, orbitals, LANES), F32)

    outgoing = pl.pallas_call(
        functools.partial(green_kernel, **sizes),
        out_shape=jax.ShapeDtypeStruct((devices * half, entries), BF),
        in_specs=[in_hbm] * 4,
        out_specs=vmem,
        scratch_shapes=[
            pltpu.SMEM(owner_counts.shape, jnp.int32),
            pltpu.VMEM((1, tiles), jnp.int32),
            pltpu.VMEM((orbitals, electrons), BF),
            pltpu.VMEM((orbitals, electrons), BF),
            wide_scratch,
            pltpu.VMEM((side * LANES, entries), BF),
            pltpu.VMEM((devices * half, tiles), BF),
            pltpu.SemaphoreType.DMA((4,)),
        ],
        compiler_params=params,
        name="green",
    )(*(in_place(x) for x in (owner_counts, pattern_row, green_factor[0], trial)))
    arrived = lax.all_to_all(
        outgoing.reshape(devices, half, entries), both, split_axis=0, concat_axis=0
    )
    partial_bias, sampled, scale = pl.pallas_call(
        functools.partial(bias_kernel, walkers=devices, half=half, block=block),
        out_shape=(
            jax.ShapeDtypeStruct((devices * lanes, LANES), BF),
            jax.ShapeDtypeStruct((lanes, LANES), F32),
            jax.ShapeDtypeStruct((lanes, LANES), F32),
        ),
        in_specs=[vmem, hbm, in_hbm, in_hbm, in_hbm],
        out_specs=(vmem,) * 3,
        scratch_shapes=[
            pltpu.VMEM((entries // LANES, half * devices, LANES), F32),
            pltpu.VMEM((devices, half * entries), BF),
            pltpu.VMEM((devices * lanes, LANES), F32),
            pltpu.VMEM((half, vectors, entries), BF),
            pltpu.VMEM(aux.shape, jnp.int32),
            pltpu.VMEM((lanes, LANES), jnp.int32),
            pltpu.SMEM(group_weight.shape, F32),
            pltpu.SemaphoreType.DMA((3,)),
            pltpu.SemaphoreType.DMA((vectors // block,)),
        ],
        compiler_params=streaming,
        cost_estimate=pl.CostEstimate(
            flops=flops, transcendentals=0, bytes_accessed=tile_bytes
        ),
        name="bias",
    )(
        arrived.reshape(devices * half, entries),
        chol,
        in_place(aux),
        in_place(chol_group.reshape(lanes, LANES)),
        in_place(group_weight),
    )
    partial_bias = lax.all_to_all(
        partial_bias.reshape(devices, lanes, LANES), both, split_axis=0, concat_axis=0
    )
    fields, summand = pl.pallas_call(
        functools.partial(field_kernel, devices=devices),
        out_shape=(
            jax.ShapeDtypeStruct((devices, lanes, LANES), BF),
            jax.ShapeDtypeStruct((lanes, LANES), F32),
        ),
        in_specs=[vmem] * 3,
        out_specs=(vmem,) * 2,
        compiler_params=params,
        name="fields",
    )(partial_bias, sampled, scale)
    fields = lax.all_to_all(fields, both, split_axis=0, concat_axis=0)
    spread_width = side * LANES
    potential, *prepared = pl.pallas_call(
        functools.partial(
            potential_kernel, walkers=devices, nblk=orbitals // side, **sizes
        ),
        out_shape=(
            jax.ShapeDtypeStruct((devices * half, entries), BF),
            jax.ShapeDtypeStruct((tiles, devices * half), BF),
            jax.ShapeDtypeStruct((entries, spread_width), BF),
            jax.ShapeDtypeStruct((LANES, tiles), BF),
            jax.ShapeDtypeStruct((tiles, LANES), F32),
        ),
        in_specs=[in_hbm, vmem, vmem, hbm],
        out_specs=(vmem,) * 5,
        scratch_shapes=[
            pltpu.VMEM((devices * lanes, LANES), F32),
            pltpu.VMEM((devices, vectors), BF),
            pltpu.VMEM((entries // LANES, half * devices, LANES), F32),
            pltpu.VMEM((half, vectors, entries), BF),
            pltpu.SMEM(owner_counts.shape, jnp.int32),
            pltpu.SemaphoreType.DMA,
            pltpu.SemaphoreType.DMA((half,)),
        ],
        compiler_params=streaming,
        cost_estimate=pl.CostEstimate(
            flops=flops, transcendentals=0, bytes_accessed=tile_bytes
        ),
        name="potential",
    )(in_place(owner_counts), pattern_row, fields.reshape(devices * lanes, LANES), chol)
    returned = lax.all_to_all(
        potential.reshape(devices, half, entries), both, split_axis=0, concat_axis=0
    )
    advanced, log_weight = pl.pallas_call(
        functools.partial(advance_kernel, side=side),
        out_shape=(
            jax.ShapeDtypeStruct((orbitals, electrons), BF),
            jax.ShapeDtypeStruct((1,), F32),
        ),
        in_specs=[vmem] * 7,
        out_specs=(vmem, smem),
        scratch_shapes=[wide_scratch],
        compiler_params=params,
        name="advance",
    )(returned.reshape(devices * half, entries), *prepared, walkers[0], summand)
    return advanced[None], log_weight


def solution(mesh):
    return jax.shard_map(
        functools.partial(
            per_device, groups=mesh.shape["groups"], owners=mesh.shape["tile"]
        ),
        mesh=mesh,
        in_specs=(
            P(("groups", "tile"), None, None),
            P(("groups", "tile"), None, None),
            P(),
            P("tile", None, None),
            P(),
            P(),
            P(),
            P(),
            P("groups", None),
        ),
        out_specs=(P(("groups", "tile"), None, None), P(("groups", "tile"))),
        check_vma=False,
    )
```

```python
import functools
import math

import jax
import jax.numpy as jnp
from jax import lax
from jax.experimental import pallas as pl
from jax.experimental.pallas import tpu as pltpu
from jax.sharding import PartitionSpec as P

BF = jnp.bfloat16
F32 = jnp.float32
LANES = 128
VMEM_LIMIT = 8 * 1024 * 1024


def log2(n):
    bits = n.bit_length() - 1
    assert 1 << bits == n
    return bits


def iota(shape, axis):
    return lax.broadcasted_iota(jnp.int32, shape, axis)


def one_hot(equal):
    return jnp.where(equal, 1.0, 0.0).astype(BF)


def mm(a, b):
    return jnp.dot(a, b, preferred_element_type=F32)


def nt(a, b):
    return lax.dot_general(a, b, (((1,), (1,)), ((), ())), preferred_element_type=F32)


def slot_of_tile(counts_ref, tiles, owners, groups, half, cap):
    tile = iota((1, tiles), 1)
    owner = jnp.zeros((1, tiles), jnp.int32)
    first = jnp.zeros((1, tiles), jnp.int32)
    offset = jnp.int32(0)
    for d in range(owners):
        offset = offset + counts_ref[d]
        past = tile >= offset
        owner = jnp.where(past, d + 1, owner)
        first = jnp.where(past, offset, first)
    place = tile - first
    slot = owner * half + place
    for x in range(1, groups):
        start = min(x * half, cap - half)
        slot = jnp.where(place >= x * half, (x * owners + owner) * half + place - start, slot)
    return slot


def row_of(pat, nblk, side):
    row_block = pat >> log2(nblk)
    col_block = pat & (nblk - 1)
    per = LANES // side
    return ((col_block >> log2(per)) << log2(nblk)) + row_block, col_block & (per - 1)


def tile_columns(pattern_ref, tiles, nblk, side):
    pat = jnp.broadcast_to(pattern_ref[...].astype(F32), (LANES, tiles)).T.astype(jnp.int32)
    return row_of(pat, nblk, side)


def green_kernel(
    counts_hbm, pattern_hbm, factor_hbm, trial_hbm, out_ref,
    counts_ref, pattern_ref, factor_ref, trial_ref, wide_ref, fold_ref, slot_ref, sems,
    *, owners, groups, half, cap, side,
):
    copies = [
        pltpu.make_async_copy(source, held, sems.at[i])
        for i, (source, held) in enumerate(
            [
                (counts_hbm, counts_ref),
                (pattern_hbm, pattern_ref),
                (factor_hbm, factor_ref),
                (trial_hbm, trial_ref),
            ]
        )
    ]
    for copy in copies:
        copy.start()
    orbitals = factor_ref.shape[0]
    nblk = orbitals // side
    tiles = pattern_ref.shape[1]
    slots = out_ref.shape[0]
    wide = orbitals // LANES
    assert wide * nblk == LANES
    src = iota(fold_ref.shape, 0)
    dst = iota(fold_ref.shape, 1)
    fold_ref[...] = one_hot(((src >> log2(LANES)) << log2(side)) + (src & (side - 1)) == dst)
    copies[0].wait()
    copies[1].wait()
    where_row, place = tile_columns(pattern_ref, tiles, nblk, side)
    lane = iota((tiles, LANES), 1)
    pick = one_hot(where_row == lane)
    inside = place == (lane >> log2(side))
    slot = slot_of_tile(counts_ref, tiles, owners, groups, half, cap)
    slot_ref[...] = one_hot(iota((slots, tiles), 0) == slot)
    copies[2].wait()
    copies[3].wait()
    green = nt(factor_ref[...], trial_ref[...])
    for k in range(wide):
        wide_ref[k] = green[:, k * LANES : (k + 1) * LANES]
    cut = jnp.concatenate(
        [
            jnp.concatenate(
                [wide_ref[k, pl.ds(p, nblk, stride=side), :] for p in range(side)], axis=1
            ).astype(BF)
            for k in range(wide)
        ],
        axis=0,
    )
    found = mm(pick, cut)
    kept = jnp.concatenate(
        [
            jnp.where(inside, found[:, p * LANES : (p + 1) * LANES], 0.0).astype(BF)
            for p in range(side)
        ],
        axis=1,
    )
    values = mm(kept, fold_ref[...]).astype(BF)
    out_ref[...] = mm(slot_ref[...], values).astype(BF)


def in_place(x):
    return pltpu.with_memory_space_constraint(x, pltpu.HBM)


def first_slot(half, cap):
    return jnp.minimum(lax.axis_index("groups") * half, cap - half)


def bias_kernel(
    green_ref, chol_ref, out_ref, tall, left, back, held, sems, *, walkers, half, block
):
    entries = green_ref.shape[1]
    vectors = held.shape[1]
    lanes = vectors // LANES
    narrow = entries // LANES
    steps = vectors // block
    first = first_slot(half, chol_ref.shape[0])

    def fetch(s):
        rows = pl.ds(s * block if isinstance(s, int) else pl.multiple_of(s * block, block), block)
        return pltpu.make_async_copy(
            chol_ref.at[pl.ds(first, half), rows, :], held.at[:, rows, :], sems.at[s]
        )

    for s in range(steps):
        fetch(s).start()
    for k in range(narrow):
        tall[k] = green_ref[:, k * LANES : (k + 1) * LANES].astype(F32)
    for j in range(half):
        for k in range(narrow):
            at = j * entries + k * LANES
            left[:, at : at + LANES] = tall[k, pl.ds(j, walkers, stride=half), :].astype(BF)

    def step(s, carry):
        fetch(s).wait()
        rows = pl.ds(pl.multiple_of(s * block, block), block)
        right = jnp.concatenate([held[j, rows, :] for j in range(half)], axis=1)
        total = nt(left[...], right)
        for i in range(block // LANES):
            place = s * (block // LANES) + i
            back[pl.ds(place, walkers, stride=lanes), :] = total[:, i * LANES : (i + 1) * LANES]
        return carry

    lax.fori_loop(0, steps, step, 0)
    out_ref[...] = back[...].astype(BF)


def field_kernel(partial_ref, aux_ref, group_ref, weight_ref, fields_ref, summand_ref, *, devices):
    lanes = group_ref.shape[0]
    bias = partial_ref[0].astype(F32)
    for i in range(1, devices):
        bias = bias + partial_ref[i].astype(F32)
    draws = aux_ref[pl.ds(lax.axis_index("tile"), 1), :]
    draws = jnp.concatenate(
        [draws[:, i * LANES : (i + 1) * LANES] for i in range(lanes)], axis=0
    )
    sampled = draws.astype(F32) * (1.0 / 262144.0)
    scale = jnp.zeros((lanes, LANES), F32)
    for k in range(weight_ref.shape[1]):
        scale = jnp.where(group_ref[...] == k, weight_ref[:, k : k + 1], scale)
    fields = (scale * (sampled - bias)).astype(BF)
    for i in range(devices):
        fields_ref[i] = fields
    summand_ref[...] = sampled * bias - 0.5 * bias * bias


def prepare(
    counts_ref, pattern_ref, place_ref, spread_ref, pick_ref, inside_ref, *, owners, groups, half, cap, side, nblk
):
    tiles, slots = place_ref.shape
    lane = iota((tiles, LANES), 1)
    slot = slot_of_tile(counts_ref, tiles, owners, groups, half, cap)
    slot = jnp.broadcast_to(slot.astype(F32), (LANES, tiles)).T.astype(jnp.int32)
    for k in range(slots // LANES):
        place_ref[:, k * LANES : (k + 1) * LANES] = one_hot(slot == lane + k * LANES)
    src = iota(spread_ref.shape, 0)
    dst = iota(spread_ref.shape, 1)
    spread_ref[...] = one_hot(((dst >> log2(LANES)) << log2(side)) + (dst & (side - 1)) == src)
    where_row, _ = row_of(pattern_ref[...], nblk, side)
    pick_ref[...] = one_hot(iota((LANES, tiles), 0) == where_row)
    _, place = tile_columns(pattern_ref, tiles, nblk, side)
    inside_ref[...] = jnp.where(place == (lane >> log2(side)), 1.0, 0.0)


def potential_kernel(
    counts_hbm, pattern_ref, fields_ref, chol_ref,
    out_ref, place_ref, spread_ref, pick_ref, inside_ref,
    tall, left, back, held, counts_ref, counts_sem, sems, *, walkers, half, **sizes,
):
    entries = held.shape[2]
    lanes = left.shape[1] // LANES
    narrow = entries // LANES
    first = first_slot(half, chol_ref.shape[0])

    def fetch(j):
        return pltpu.make_async_copy(chol_ref.at[first + j], held.at[j], sems.at[j])

    def begin(j, carry):
        fetch(j).start()
        return carry

    counts = pltpu.make_async_copy(counts_hbm, counts_ref, counts_sem)
    counts.start()
    lax.fori_loop(0, half, begin, 0)
    counts.wait()
    prepare(
        counts_ref, pattern_ref, place_ref, spread_ref, pick_ref, inside_ref, half=half, **sizes
    )
    tall[...] = fields_ref[...].astype(F32)
    for i in range(lanes):
        left[:, i * LANES : (i + 1) * LANES] = tall[pl.ds(i, walkers, stride=lanes), :].astype(BF)

    def step(j, carry):
        fetch(j).wait()
        tile = mm(left[...], held[j])
        for k in range(narrow):
            back[k, pl.ds(j, walkers, stride=half), :] = tile[:, k * LANES : (k + 1) * LANES]
        return carry

    lax.fori_loop(0, half, step, 0)
    for k in range(narrow):
        out_ref[:, k * LANES : (k + 1) * LANES] = back[k].astype(BF)


def advance_kernel(
    tiles_ref, place_ref, spread_ref, pick_ref, inside_ref, walker_ref, summand_ref,
    out_ref, logw_ref, wide_ref, *, side,
):
    logw_ref[0] = jnp.sum(summand_ref[...])
    orbitals = walker_ref.shape[0]
    nblk = orbitals // side
    wide = orbitals // LANES
    values = mm(place_ref[...], tiles_ref[...]).astype(BF)
    repeated = mm(values, spread_ref[...])
    inside = inside_ref[...]
    kept = jnp.concatenate(
        [(repeated[:, p * LANES : (p + 1) * LANES] * inside).astype(BF) for p in range(side)],
        axis=1,
    )
    cut = mm(pick_ref[...], kept)
    for k in range(wide):
        for p in range(side):
            wide_ref[k, pl.ds(p, nblk, stride=side), :] = cut[
                k * nblk : (k + 1) * nblk, p * LANES : (p + 1) * LANES
            ]
    potential = jnp.concatenate([wide_ref[k].astype(BF) for k in range(wide)], axis=1)
    term = walker_ref[...]
    running = term.astype(F32)
    for degree in range(1, 5):
        term = (mm(potential, term) / degree).astype(BF)
        running = running + term.astype(F32)
    out_ref[...] = running.astype(BF)


def per_device(
    walkers, green_factor, trial, chol, pattern, owner_counts, chol_group, group_weight, aux, *, groups, owners
):
    devices = groups * owners
    walk_dev, orbitals, electrons = walkers.shape
    assert walk_dev == 1
    cap, vectors, entries = chol.shape
    side = math.isqrt(entries)
    lanes = vectors // LANES
    half = -(-cap // groups)
    tiles = pattern.shape[0]
    both = ("groups", "tile")
    pattern_row = pattern.reshape(1, tiles)

    smem = pl.BlockSpec(memory_space=pltpu.SMEM)
    vmem = pl.BlockSpec(memory_space=pltpu.VMEM)
    params = pltpu.CompilerParams(vmem_limit_bytes=VMEM_LIMIT)
    hbm = pl.BlockSpec(memory_space=pl.ANY)
    in_hbm = pl.BlockSpec(memory_space=pltpu.HBM)
    streaming = pltpu.CompilerParams(
        vmem_limit_bytes=VMEM_LIMIT + 2 * half * vectors * entries
    )
    sizes = dict(owners=owners, groups=groups, half=half, cap=cap, side=side)
    block = min(256, vectors)
    tile_bytes = half * vectors * entries * 2
    flops = 2 * devices * half * vectors * entries
    wide_scratch = pltpu.VMEM((orbitals // LANES, orbitals, LANES), F32)

    outgoing = pl.pallas_call(
        functools.partial(green_kernel, **sizes),
        out_shape=jax.ShapeDtypeStruct((devices * half, entries), BF),
        in_specs=[in_hbm] * 4,
        out_specs=vmem,
        scratch_shapes=[
            pltpu.SMEM(owner_counts.shape, jnp.int32),
            pltpu.VMEM((1, tiles), jnp.int32),
            pltpu.VMEM((orbitals, electrons), BF),
            pltpu.VMEM((orbitals, electrons), BF),
            wide_scratch,
            pltpu.VMEM((side * LANES, entries), BF),
            pltpu.VMEM((devices * half, tiles), BF),
            pltpu.SemaphoreType.DMA((4,)),
        ],
        compiler_params=params,
        name="green",
    )(*(in_place(x) for x in (owner_counts, pattern_row, green_factor[0], trial)))
    arrived = lax.all_to_all(
        outgoing.reshape(devices, half, entries), both, split_axis=0, concat_axis=0
    )
    partial_bias = pl.pallas_call(
        functools.partial(bias_kernel, walkers=devices, half=half, block=block),
        out_shape=jax.ShapeDtypeStruct((devices * lanes, LANES), BF),
        in_specs=[vmem, hbm],
        out_specs=vmem,
        scratch_shapes=[
            pltpu.VMEM((entries // LANES, half * devices, LANES), F32),
            pltpu.VMEM((devices, half * entries), BF),
            pltpu.VMEM((devices * lanes, LANES), F32),
            pltpu.VMEM((half, vectors, entries), BF),
            pltpu.SemaphoreType.DMA((vectors // block,)),
        ],
        compiler_params=streaming,
        cost_estimate=pl.CostEstimate(
            flops=flops, transcendentals=0, bytes_accessed=tile_bytes
        ),
        name="bias",
    )(arrived.reshape(devices * half, entries), chol)
    partial_bias = lax.all_to_all(
        partial_bias.reshape(devices, lanes, LANES), both, split_axis=0, concat_axis=0
    )
    fields, summand = pl.pallas_call(
        functools.partial(field_kernel, devices=devices),
        out_shape=(
            jax.ShapeDtypeStruct((devices, lanes, LANES), BF),
            jax.ShapeDtypeStruct((lanes, LANES), F32),
        ),
        in_specs=[vmem] * 4,
        out_specs=(vmem,) * 2,
        compiler_params=params,
        name="fields",
    )(partial_bias, aux, chol_group.reshape(lanes, LANES), group_weight.reshape(1, -1))
    fields = lax.all_to_all(fields, both, split_axis=0, concat_axis=0)
    spread_width = side * LANES
    potential, *prepared = pl.pallas_call(
        functools.partial(
            potential_kernel, walkers=devices, nblk=orbitals // side, **sizes
        ),
        out_shape=(
            jax.ShapeDtypeStruct((devices * half, entries), BF),
            jax.ShapeDtypeStruct((tiles, devices * half), BF),
            jax.ShapeDtypeStruct((entries, spread_width), BF),
            jax.ShapeDtypeStruct((LANES, tiles), BF),
            jax.ShapeDtypeStruct((tiles, LANES), F32),
        ),
        in_specs=[in_hbm, vmem, vmem, hbm],
        out_specs=(vmem,) * 5,
        scratch_shapes=[
            pltpu.VMEM((devices * lanes, LANES), F32),
            pltpu.VMEM((devices, vectors), BF),
            pltpu.VMEM((entries // LANES, half * devices, LANES), F32),
            pltpu.VMEM((half, vectors, entries), BF),
            pltpu.SMEM(owner_counts.shape, jnp.int32),
            pltpu.SemaphoreType.DMA,
            pltpu.SemaphoreType.DMA((half,)),
        ],
        compiler_params=streaming,
        cost_estimate=pl.CostEstimate(
            flops=flops, transcendentals=0, bytes_accessed=tile_bytes
        ),
        name="potential",
    )(in_place(owner_counts), pattern_row, fields.reshape(devices * lanes, LANES), chol)
    returned = lax.all_to_all(
        potential.reshape(devices, half, entries), both, split_axis=0, concat_axis=0
    )
    advanced, log_weight = pl.pallas_call(
        functools.partial(advance_kernel, side=side),
        out_shape=(
            jax.ShapeDtypeStruct((orbitals, electrons), BF),
            jax.ShapeDtypeStruct((1,), F32),
        ),
        in_specs=[vmem] * 7,
        out_specs=(vmem, smem),
        scratch_shapes=[wide_scratch],
        compiler_params=params,
        name="advance",
    )(returned.reshape(devices * half, entries), *prepared, walkers[0], summand)
    return advanced[None], log_weight


def solution(mesh):
    return jax.shard_map(
        functools.partial(
            per_device, groups=mesh.shape["groups"], owners=mesh.shape["tile"]
        ),
        mesh=mesh,
        in_specs=(
            P(("groups", "tile"), None, None),
            P(("groups", "tile"), None, None),
            P(),
            P("tile", None, None),
            P(),
            P(),
            P(),
            P(),
            P("groups", None),
        ),
        out_specs=(P(("groups", "tile"), None, None), P(("groups", "tile"))),
        check_vma=False,
    )
```

```python
import functools
import math

import jax
import jax.numpy as jnp
from jax import lax
from jax.experimental import pallas as pl
from jax.experimental.pallas import tpu as pltpu
from jax.sharding import PartitionSpec as P

BF = jnp.bfloat16
F32 = jnp.float32
LANES = 128
VMEM_LIMIT = 8 * 1024 * 1024


def log2(n):
    bits = n.bit_length() - 1
    assert 1 << bits == n
    return bits


def iota(shape, axis):
    return lax.broadcasted_iota(jnp.int32, shape, axis)


def one_hot(equal):
    return jnp.where(equal, 1.0, 0.0).astype(BF)


def mm(a, b):
    return jnp.dot(a, b, preferred_element_type=F32)


def nt(a, b):
    return lax.dot_general(a, b, (((1,), (1,)), ((), ())), preferred_element_type=F32)


def slot_of_tile(counts_ref, tiles, owners, groups, half, cap):
    tile = iota((1, tiles), 1)
    owner = jnp.zeros((1, tiles), jnp.int32)
    first = jnp.zeros((1, tiles), jnp.int32)
    offset = jnp.int32(0)
    for d in range(owners):
        offset = offset + counts_ref[d]
        past = tile >= offset
        owner = jnp.where(past, d + 1, owner)
        first = jnp.where(past, offset, first)
    place = tile - first
    slot = owner * half + place
    for x in range(1, groups):
        start = min(x * half, cap - half)
        slot = jnp.where(place >= x * half, (x * owners + owner) * half + place - start, slot)
    return slot


def row_of(pat, nblk, side):
    row_block = pat >> log2(nblk)
    col_block = pat & (nblk - 1)
    per = LANES // side
    return ((col_block >> log2(per)) << log2(nblk)) + row_block, col_block & (per - 1)


def tile_columns(pattern_ref, tiles, nblk, side):
    pat = jnp.broadcast_to(pattern_ref[...].astype(F32), (LANES, tiles)).T.astype(jnp.int32)
    return row_of(pat, nblk, side)


def green_kernel(
    counts_hbm, pattern_hbm, factor_hbm, trial_hbm, out_ref,
    counts_ref, pattern_ref, factor_ref, trial_ref, wide_ref, fold_ref, slot_ref, sems,
    *, owners, groups, half, cap, side,
):
    copies = [
        pltpu.make_async_copy(source, held, sems.at[i])
        for i, (source, held) in enumerate(
            [
                (counts_hbm, counts_ref),
                (pattern_hbm, pattern_ref),
                (factor_hbm, factor_ref),
                (trial_hbm, trial_ref),
            ]
        )
    ]
    for copy in copies:
        copy.start()
    orbitals = factor_ref.shape[0]
    nblk = orbitals // side
    tiles = pattern_ref.shape[1]
    slots = out_ref.shape[0]
    wide = orbitals // LANES
    assert wide * nblk == LANES
    src = iota(fold_ref.shape, 0)
    dst = iota(fold_ref.shape, 1)
    fold_ref[...] = one_hot(((src >> log2(LANES)) << log2(side)) + (src & (side - 1)) == dst)
    copies[0].wait()
    copies[1].wait()
    where_row, place = tile_columns(pattern_ref, tiles, nblk, side)
    lane = iota((tiles, LANES), 1)
    pick = one_hot(where_row == lane)
    inside = place == (lane >> log2(side))
    slot = slot_of_tile(counts_ref, tiles, owners, groups, half, cap)
    slot_ref[...] = one_hot(iota((slots, tiles), 0) == slot)
    copies[2].wait()
    copies[3].wait()
    green = nt(factor_ref[...], trial_ref[...])
    for k in range(wide):
        wide_ref[k] = green[:, k * LANES : (k + 1) * LANES]
    values = jnp.zeros((tiles, side * side), F32)
    count = 2
    for g in range(side // count):
        cut = jnp.concatenate(
            [
                jnp.concatenate(
                    [
                        wide_ref[k, pl.ds(g * count + p, nblk, stride=side), :]
                        for p in range(count)
                    ],
                    axis=1,
                ).astype(BF)
                for k in range(wide)
            ],
            axis=0,
        )
        found = mm(pick, cut)
        kept = jnp.concatenate(
            [
                jnp.where(inside, found[:, p * LANES : (p + 1) * LANES], 0.0).astype(BF)
                for p in range(count)
            ],
            axis=1,
        )
        span = count * LANES
        values = values + mm(kept, fold_ref[g * span : (g + 1) * span, :])
    values = values.astype(BF)
    out_ref[...] = mm(slot_ref[...], values).astype(BF)


def in_place(x):
    return pltpu.with_memory_space_constraint(x, pltpu.HBM)


def first_slot(half, cap):
    return jnp.minimum(lax.axis_index("groups") * half, cap - half)


def bias_kernel(
    green_ref, chol_ref, out_ref, tall, left, back, held, sems, *, walkers, half, block
):
    entries = green_ref.shape[1]
    vectors = held.shape[1]
    lanes = vectors // LANES
    narrow = entries // LANES
    steps = vectors // block
    first = first_slot(half, chol_ref.shape[0])

    def fetch(s):
        rows = pl.ds(s * block if isinstance(s, int) else pl.multiple_of(s * block, block), block)
        return pltpu.make_async_copy(
            chol_ref.at[pl.ds(first, half), rows, :], held.at[:, rows, :], sems.at[s]
        )

    for s in range(steps):
        fetch(s).start()
    for k in range(narrow):
        tall[k] = green_ref[:, k * LANES : (k + 1) * LANES].astype(F32)
    for j in range(half):
        for k in range(narrow):
            at = j * entries + k * LANES
            left[:, at : at + LANES] = tall[k, pl.ds(j, walkers, stride=half), :].astype(BF)

    def step(s, carry):
        fetch(s).wait()
        rows = pl.ds(pl.multiple_of(s * block, block), block)
        right = jnp.concatenate([held[j, rows, :] for j in range(half)], axis=1)
        total = nt(left[...], right)
        for i in range(block // LANES):
            place = s * (block // LANES) + i
            back[pl.ds(place, walkers, stride=lanes), :] = total[:, i * LANES : (i + 1) * LANES]
        return carry

    lax.fori_loop(0, steps, step, 0)
    out_ref[...] = back[...].astype(BF)


def field_kernel(partial_ref, aux_ref, group_ref, weight_ref, fields_ref, summand_ref, *, devices):
    lanes = group_ref.shape[0]
    bias = partial_ref[0].astype(F32)
    for i in range(1, devices):
        bias = bias + partial_ref[i].astype(F32)
    draws = aux_ref[pl.ds(lax.axis_index("tile"), 1), :]
    draws = jnp.concatenate(
        [draws[:, i * LANES : (i + 1) * LANES] for i in range(lanes)], axis=0
    )
    sampled = draws.astype(F32) * (1.0 / 262144.0)
    scale = jnp.zeros((lanes, LANES), F32)
    for k in range(weight_ref.shape[1]):
        scale = jnp.where(group_ref[...] == k, weight_ref[:, k : k + 1], scale)
    fields = (scale * (sampled - bias)).astype(BF)
    for i in range(devices):
        fields_ref[i] = fields
    summand_ref[...] = sampled * bias - 0.5 * bias * bias


def prepare(
    counts_ref, pattern_ref, place_ref, spread_ref, pick_ref, inside_ref, *, owners, groups, half, cap, side, nblk
):
    tiles, slots = place_ref.shape
    lane = iota((tiles, LANES), 1)
    slot = slot_of_tile(counts_ref, tiles, owners, groups, half, cap)
    slot = jnp.broadcast_to(slot.astype(F32), (LANES, tiles)).T.astype(jnp.int32)
    for k in range(slots // LANES):
        place_ref[:, k * LANES : (k + 1) * LANES] = one_hot(slot == lane + k * LANES)
    src = iota(spread_ref.shape, 0)
    dst = iota(spread_ref.shape, 1)
    spread_ref[...] = one_hot(((dst >> log2(LANES)) << log2(side)) + (dst & (side - 1)) == src)
    where_row, _ = row_of(pattern_ref[...], nblk, side)
    pick_ref[...] = one_hot(iota((LANES, tiles), 0) == where_row)
    _, place = tile_columns(pattern_ref, tiles, nblk, side)
    inside_ref[...] = jnp.where(place == (lane >> log2(side)), 1.0, 0.0)


def potential_kernel(
    counts_hbm, pattern_ref, fields_ref, chol_ref,
    out_ref, place_ref, spread_ref, pick_ref, inside_ref,
    tall, left, back, held, counts_ref, counts_sem, sems, *, walkers, half, **sizes,
):
    entries = held.shape[2]
    lanes = left.shape[1] // LANES
    narrow = entries // LANES
    first = first_slot(half, chol_ref.shape[0])

    def fetch(j):
        return pltpu.make_async_copy(chol_ref.at[first + j], held.at[j], sems.at[j])

    def begin(j, carry):
        fetch(j).start()
        return carry

    counts = pltpu.make_async_copy(counts_hbm, counts_ref, counts_sem)
    counts.start()
    lax.fori_loop(0, half, begin, 0)
    counts.wait()
    prepare(
        counts_ref, pattern_ref, place_ref, spread_ref, pick_ref, inside_ref, half=half, **sizes
    )
    tall[...] = fields_ref[...].astype(F32)
    for i in range(lanes):
        left[:, i * LANES : (i + 1) * LANES] = tall[pl.ds(i, walkers, stride=lanes), :].astype(BF)

    def step(j, carry):
        fetch(j).wait()
        tile = mm(left[...], held[j])
        for k in range(narrow):
            back[k, pl.ds(j, walkers, stride=half), :] = tile[:, k * LANES : (k + 1) * LANES]
        return carry

    lax.fori_loop(0, half, step, 0)
    for k in range(narrow):
        out_ref[:, k * LANES : (k + 1) * LANES] = back[k].astype(BF)


def advance_kernel(
    tiles_ref, place_ref, spread_ref, pick_ref, inside_ref, walker_ref, summand_ref,
    out_ref, logw_ref, wide_ref, *, side,
):
    logw_ref[0] = jnp.sum(summand_ref[...])
    orbitals = walker_ref.shape[0]
    nblk = orbitals // side
    wide = orbitals // LANES
    values = mm(place_ref[...], tiles_ref[...]).astype(BF)
    repeated = mm(values, spread_ref[...])
    inside = inside_ref[...]
    kept = jnp.concatenate(
        [(repeated[:, p * LANES : (p + 1) * LANES] * inside).astype(BF) for p in range(side)],
        axis=1,
    )
    cut = mm(pick_ref[...], kept)
    for k in range(wide):
        for p in range(side):
            wide_ref[k, pl.ds(p, nblk, stride=side), :] = cut[
                k * nblk : (k + 1) * nblk, p * LANES : (p + 1) * LANES
            ]
    potential = jnp.concatenate([wide_ref[k].astype(BF) for k in range(wide)], axis=1)
    terms = [walker_ref[...]]
    rows = orbitals // 2
    for degree in range(1, 5):
        term = [
            (mm(potential[i * rows : (i + 1) * rows], terms[-1]) / degree).astype(BF)
            for i in range(2)
        ]
        terms.append(jnp.concatenate(term, axis=0))
    running = terms[0].astype(F32)
    for term in terms[1:]:
        running = running + term.astype(F32)
    out_ref[...] = running.astype(BF)


def per_device(
    walkers, green_factor, trial, chol, pattern, owner_counts, chol_group, group_weight, aux, *, groups, owners
):
    devices = groups * owners
    walk_dev, orbitals, electrons = walkers.shape
    assert walk_dev == 1
    cap, vectors, entries = chol.shape
    side = math.isqrt(entries)
    lanes = vectors // LANES
    half = -(-cap // groups)
    tiles = pattern.shape[0]
    both = ("groups", "tile")
    pattern_row = pattern.reshape(1, tiles)

    smem = pl.BlockSpec(memory_space=pltpu.SMEM)
    vmem = pl.BlockSpec(memory_space=pltpu.VMEM)
    params = pltpu.CompilerParams(vmem_limit_bytes=VMEM_LIMIT)
    hbm = pl.BlockSpec(memory_space=pl.ANY)
    in_hbm = pl.BlockSpec(memory_space=pltpu.HBM)
    streaming = pltpu.CompilerParams(
        vmem_limit_bytes=VMEM_LIMIT + 2 * half * vectors * entries
    )
    sizes = dict(owners=owners, groups=groups, half=half, cap=cap, side=side)
    block = min(256, vectors)
    tile_bytes = half * vectors * entries * 2
    flops = 2 * devices * half * vectors * entries
    wide_scratch = pltpu.VMEM((orbitals // LANES, orbitals, LANES), F32)

    outgoing = pl.pallas_call(
        functools.partial(green_kernel, **sizes),
        out_shape=jax.ShapeDtypeStruct((devices * half, entries), BF),
        in_specs=[in_hbm] * 4,
        out_specs=vmem,
        scratch_shapes=[
            pltpu.SMEM(owner_counts.shape, jnp.int32),
            pltpu.VMEM((1, tiles), jnp.int32),
            pltpu.VMEM((orbitals, electrons), BF),
            pltpu.VMEM((orbitals, electrons), BF),
            wide_scratch,
            pltpu.VMEM((side * LANES, entries), BF),
            pltpu.VMEM((devices * half, tiles), BF),
            pltpu.SemaphoreType.DMA((4,)),
        ],
        compiler_params=params,
        name="green",
    )(*(in_place(x) for x in (owner_counts, pattern_row, green_factor[0], trial)))
    arrived = lax.all_to_all(
        outgoing.reshape(devices, half, entries), both, split_axis=0, concat_axis=0
    )
    partial_bias = pl.pallas_call(
        functools.partial(bias_kernel, walkers=devices, half=half, block=block),
        out_shape=jax.ShapeDtypeStruct((devices * lanes, LANES), BF),
        in_specs=[vmem, hbm],
        out_specs=vmem,
        scratch_shapes=[
            pltpu.VMEM((entries // LANES, half * devices, LANES), F32),
            pltpu.VMEM((devices, half * entries), BF),
            pltpu.VMEM((devices * lanes, LANES), F32),
            pltpu.VMEM((half, vectors, entries), BF),
            pltpu.SemaphoreType.DMA((vectors // block,)),
        ],
        compiler_params=streaming,
        cost_estimate=pl.CostEstimate(
            flops=flops, transcendentals=0, bytes_accessed=tile_bytes
        ),
        name="bias",
    )(arrived.reshape(devices * half, entries), chol)
    partial_bias = lax.all_to_all(
        partial_bias.reshape(devices, lanes, LANES), both, split_axis=0, concat_axis=0
    )
    fields, summand = pl.pallas_call(
        functools.partial(field_kernel, devices=devices),
        out_shape=(
            jax.ShapeDtypeStruct((devices, lanes, LANES), BF),
            jax.ShapeDtypeStruct((lanes, LANES), F32),
        ),
        in_specs=[vmem] * 4,
        out_specs=(vmem,) * 2,
        compiler_params=params,
        name="fields",
    )(partial_bias, aux, chol_group.reshape(lanes, LANES), group_weight.reshape(1, -1))
    fields = lax.all_to_all(fields, both, split_axis=0, concat_axis=0)
    spread_width = side * LANES
    potential, *prepared = pl.pallas_call(
        functools.partial(
            potential_kernel, walkers=devices, nblk=orbitals // side, **sizes
        ),
        out_shape=(
            jax.ShapeDtypeStruct((devices * half, entries), BF),
            jax.ShapeDtypeStruct((tiles, devices * half), BF),
            jax.ShapeDtypeStruct((entries, spread_width), BF),
            jax.ShapeDtypeStruct((LANES, tiles), BF),
            jax.ShapeDtypeStruct((tiles, LANES), F32),
        ),
        in_specs=[in_hbm, vmem, vmem, hbm],
        out_specs=(vmem,) * 5,
        scratch_shapes=[
            pltpu.VMEM((devices * lanes, LANES), F32),
            pltpu.VMEM((devices, vectors), BF),
            pltpu.VMEM((entries // LANES, half * devices, LANES), F32),
            pltpu.VMEM((half, vectors, entries), BF),
            pltpu.SMEM(owner_counts.shape, jnp.int32),
            pltpu.SemaphoreType.DMA,
            pltpu.SemaphoreType.DMA((half,)),
        ],
        compiler_params=streaming,
        cost_estimate=pl.CostEstimate(
            flops=flops, transcendentals=0, bytes_accessed=tile_bytes
        ),
        name="potential",
    )(in_place(owner_counts), pattern_row, fields.reshape(devices * lanes, LANES), chol)
    returned = lax.all_to_all(
        potential.reshape(devices, half, entries), both, split_axis=0, concat_axis=0
    )
    advanced, log_weight = pl.pallas_call(
        functools.partial(advance_kernel, side=side),
        out_shape=(
            jax.ShapeDtypeStruct((orbitals, electrons), BF),
            jax.ShapeDtypeStruct((1,), F32),
        ),
        in_specs=[vmem] * 7,
        out_specs=(vmem, smem),
        scratch_shapes=[wide_scratch],
        compiler_params=params,
        name="advance",
    )(returned.reshape(devices * half, entries), *prepared, walkers[0], summand)
    return advanced[None], log_weight


def solution(mesh):
    return jax.shard_map(
        functools.partial(
            per_device, groups=mesh.shape["groups"], owners=mesh.shape["tile"]
        ),
        mesh=mesh,
        in_specs=(
            P(("groups", "tile"), None, None),
            P(("groups", "tile"), None, None),
            P(),
            P("tile", None, None),
            P(),
            P(),
            P(),
            P(),
            P("groups", None),
        ),
        out_specs=(P(("groups", "tile"), None, None), P(("groups", "tile"))),
        check_vma=False,
    )
```

```python
import functools
import math

import jax
import jax.numpy as jnp
from jax import lax
from jax.experimental import pallas as pl
from jax.experimental.pallas import tpu as pltpu
from jax.sharding import PartitionSpec as P

BF = jnp.bfloat16
F32 = jnp.float32
LANES = 128
VMEM_LIMIT = 8 * 1024 * 1024


def log2(n):
    bits = n.bit_length() - 1
    assert 1 << bits == n
    return bits


def iota(shape, axis):
    return lax.broadcasted_iota(jnp.int32, shape, axis)


def one_hot(equal):
    return jnp.where(equal, 1.0, 0.0).astype(BF)


def mm(a, b):
    return jnp.dot(a, b, preferred_element_type=F32)


def nt(a, b):
    return lax.dot_general(a, b, (((1,), (1,)), ((), ())), preferred_element_type=F32)


def tn(a, b):
    return lax.dot_general(a, b, (((0,), (0,)), ((), ())), preferred_element_type=F32)


def slot_of_tile(counts_ref, tiles, owners, groups, half, cap):
    tile = iota((1, tiles), 1)
    owner = jnp.zeros((1, tiles), jnp.int32)
    first = jnp.zeros((1, tiles), jnp.int32)
    offset = jnp.int32(0)
    for d in range(owners):
        offset = offset + counts_ref[d]
        past = tile >= offset
        owner = jnp.where(past, d + 1, owner)
        first = jnp.where(past, offset, first)
    place = tile - first
    slot = owner * half + place
    for x in range(1, groups):
        start = min(x * half, cap - half)
        slot = jnp.where(place >= x * half, (x * owners + owner) * half + place - start, slot)
    return slot


def row_of(pat, nblk, side):
    row_block = pat >> log2(nblk)
    col_block = pat & (nblk - 1)
    per = LANES // side
    return ((col_block >> log2(per)) << log2(nblk)) + row_block, col_block & (per - 1)


def tile_columns(pattern_ref, tiles, nblk, side):
    pat = jnp.broadcast_to(pattern_ref[...].astype(F32), (LANES, tiles)).T.astype(jnp.int32)
    return row_of(pat, nblk, side)


def green_kernel(
    counts_hbm, pattern_hbm, factor_hbm, trial_hbm,
    out_ref, fold_ref, slot_ref, pick_ref, inside_ref,
    counts_ref, pattern_ref, factor_ref, trial_ref, wide_ref, sems,
    *, owners, groups, half, cap, side,
):
    copies = [
        pltpu.make_async_copy(source, held, sems.at[i])
        for i, (source, held) in enumerate(
            [
                (counts_hbm, counts_ref),
                (pattern_hbm, pattern_ref),
                (factor_hbm, factor_ref),
                (trial_hbm, trial_ref),
            ]
        )
    ]
    for copy in copies:
        copy.start()
    orbitals = factor_ref.shape[0]
    nblk = orbitals // side
    tiles = pattern_ref.shape[1]
    slots = out_ref.shape[0]
    wide = orbitals // LANES
    assert wide * nblk == LANES
    src = iota(fold_ref.shape, 0)
    dst = iota(fold_ref.shape, 1)
    fold_ref[...] = one_hot(((src >> log2(LANES)) << log2(side)) + (src & (side - 1)) == dst)
    copies[0].wait()
    copies[1].wait()
    where_row, place = tile_columns(pattern_ref, tiles, nblk, side)
    lane = iota((tiles, LANES), 1)
    pick = one_hot(where_row == lane)
    inside = place == (lane >> log2(side))
    pick_ref[...] = pick
    inside_ref[...] = jnp.where(inside, 1.0, 0.0)
    slot = slot_of_tile(counts_ref, tiles, owners, groups, half, cap)
    slot_ref[...] = one_hot(iota((slots, tiles), 0) == slot)
    copies[2].wait()
    copies[3].wait()
    green = nt(factor_ref[...], trial_ref[...])
    for k in range(wide):
        wide_ref[k] = green[:, k * LANES : (k + 1) * LANES]
    values = jnp.zeros((tiles, side * side), F32)
    count = 2
    for g in range(side // count):
        cut = jnp.concatenate(
            [
                jnp.concatenate(
                    [
                        wide_ref[k, pl.ds(g * count + p, nblk, stride=side), :]
                        for p in range(count)
                    ],
                    axis=1,
                ).astype(BF)
                for k in range(wide)
            ],
            axis=0,
        )
        found = mm(pick, cut)
        kept = jnp.concatenate(
            [
                jnp.where(inside, found[:, p * LANES : (p + 1) * LANES], 0.0).astype(BF)
                for p in range(count)
            ],
            axis=1,
        )
        span = count * LANES
        values = values + mm(kept, fold_ref[g * span : (g + 1) * span, :])
    values = values.astype(BF)
    out_ref[...] = mm(slot_ref[...], values).astype(BF)


def in_place(x):
    return pltpu.with_memory_space_constraint(x, pltpu.HBM)


def first_slot(half, cap):
    return jnp.minimum(lax.axis_index("groups") * half, cap - half)


def bias_kernel(
    green_ref, chol_ref, out_ref, held, tall, left, back, sems, *, walkers, half, block
):
    entries = green_ref.shape[1]
    vectors = held.shape[1]
    lanes = vectors // LANES
    narrow = entries // LANES
    steps = vectors // block
    first = first_slot(half, chol_ref.shape[0])

    def fetch(s):
        rows = pl.ds(s * block if isinstance(s, int) else pl.multiple_of(s * block, block), block)
        return pltpu.make_async_copy(
            chol_ref.at[pl.ds(first, half), rows, :], held.at[:, rows, :], sems.at[s]
        )

    for s in range(steps):
        fetch(s).start()
    for k in range(narrow):
        tall[k] = green_ref[:, k * LANES : (k + 1) * LANES].astype(F32)
    for j in range(half):
        for k in range(narrow):
            at = j * entries + k * LANES
            left[:, at : at + LANES] = tall[k, pl.ds(j, walkers, stride=half), :].astype(BF)

    def step(s, carry):
        fetch(s).wait()
        rows = pl.ds(pl.multiple_of(s * block, block), block)
        right = jnp.concatenate([held[j, rows, :] for j in range(half)], axis=1)
        total = nt(left[...], right)
        for i in range(block // LANES):
            place = s * (block // LANES) + i
            back[pl.ds(place, walkers, stride=lanes), :] = total[:, i * LANES : (i + 1) * LANES]
        return carry

    lax.fori_loop(0, steps, step, 0)
    out_ref[...] = back[...].astype(BF)


def field_kernel(partial_ref, aux_ref, group_ref, weight_ref, fields_ref, summand_ref, *, devices):
    lanes = group_ref.shape[0]
    bias = partial_ref[0].astype(F32)
    for i in range(1, devices):
        bias = bias + partial_ref[i].astype(F32)
    draws = aux_ref[pl.ds(lax.axis_index("tile"), 1), :]
    draws = jnp.concatenate(
        [draws[:, i * LANES : (i + 1) * LANES] for i in range(lanes)], axis=0
    )
    sampled = draws.astype(F32) * (1.0 / 262144.0)
    scale = jnp.zeros((lanes, LANES), F32)
    for k in range(weight_ref.shape[1]):
        scale = jnp.where(group_ref[...] == k, weight_ref[:, k : k + 1], scale)
    fields = (scale * (sampled - bias)).astype(BF)
    for i in range(devices):
        fields_ref[i] = fields
    summand_ref[...] = sampled * bias - 0.5 * bias * bias


def potential_kernel(fields_ref, held, out_ref, tall, left, back, *, walkers, half):
    entries = held.shape[2]
    lanes = left.shape[1] // LANES
    narrow = entries // LANES
    tall[...] = fields_ref[...].astype(F32)
    for i in range(lanes):
        left[:, i * LANES : (i + 1) * LANES] = tall[pl.ds(i, walkers, stride=lanes), :].astype(BF)
    count = 4 if half % 4 == 0 else 1

    def step(s, carry):
        for i in range(count):
            j = s * count + i
            tile = mm(left[...], held[j])
            for k in range(narrow):
                back[k, pl.ds(j, walkers, stride=half), :] = tile[:, k * LANES : (k + 1) * LANES]
        return carry

    lax.fori_loop(0, half // count, step, 0)
    for k in range(narrow):
        out_ref[:, k * LANES : (k + 1) * LANES] = back[k].astype(BF)


def advance_kernel(
    tiles_ref, fold_ref, slot_ref, pick_ref, inside_ref, walker_ref, summand_ref,
    out_ref, logw_ref, wide_ref, *, side,
):
    logw_ref[0] = jnp.sum(summand_ref[...])
    orbitals = walker_ref.shape[0]
    nblk = orbitals // side
    wide = orbitals // LANES
    values = tn(slot_ref[...], tiles_ref[...]).astype(BF)
    repeated = nt(values, fold_ref[...])
    inside = inside_ref[...]
    kept = jnp.concatenate(
        [(repeated[:, p * LANES : (p + 1) * LANES] * inside).astype(BF) for p in range(side)],
        axis=1,
    )
    cut = tn(pick_ref[...], kept)
    for k in range(wide):
        for p in range(side):
            wide_ref[k, pl.ds(p, nblk, stride=side), :] = cut[
                k * nblk : (k + 1) * nblk, p * LANES : (p + 1) * LANES
            ]
    potential = jnp.concatenate([wide_ref[k].astype(BF) for k in range(wide)], axis=1)
    terms = [walker_ref[...]]
    rows = orbitals // 2
    for degree in range(1, 5):
        term = [
            (mm(potential[i * rows : (i + 1) * rows], terms[-1]) / degree).astype(BF)
            for i in range(2)
        ]
        terms.append(jnp.concatenate(term, axis=0))
    running = terms[0].astype(F32)
    for term in terms[1:]:
        running = running + term.astype(F32)
    out_ref[...] = running.astype(BF)


def per_device(
    walkers, green_factor, trial, chol, pattern, owner_counts, chol_group, group_weight, aux, *, groups, owners
):
    devices = groups * owners
    walk_dev, orbitals, electrons = walkers.shape
    assert walk_dev == 1
    cap, vectors, entries = chol.shape
    side = math.isqrt(entries)
    lanes = vectors // LANES
    half = -(-cap // groups)
    tiles = pattern.shape[0]
    both = ("groups", "tile")
    pattern_row = pattern.reshape(1, tiles)

    smem = pl.BlockSpec(memory_space=pltpu.SMEM)
    vmem = pl.BlockSpec(memory_space=pltpu.VMEM)
    params = pltpu.CompilerParams(vmem_limit_bytes=VMEM_LIMIT)
    hbm = pl.BlockSpec(memory_space=pl.ANY)
    in_hbm = pl.BlockSpec(memory_space=pltpu.HBM)
    streaming = pltpu.CompilerParams(
        vmem_limit_bytes=VMEM_LIMIT + 2 * half * vectors * entries
    )
    sizes = dict(owners=owners, groups=groups, half=half, cap=cap, side=side)
    block = min(256, vectors)
    tile_bytes = half * vectors * entries * 2
    flops = 2 * devices * half * vectors * entries
    wide_scratch = pltpu.VMEM((orbitals // LANES, orbitals, LANES), F32)

    outgoing, *choices = pl.pallas_call(
        functools.partial(green_kernel, **sizes),
        out_shape=(
            jax.ShapeDtypeStruct((devices * half, entries), BF),
            jax.ShapeDtypeStruct((side * LANES, entries), BF),
            jax.ShapeDtypeStruct((devices * half, tiles), BF),
            jax.ShapeDtypeStruct((tiles, LANES), BF),
            jax.ShapeDtypeStruct((tiles, LANES), F32),
        ),
        in_specs=[in_hbm] * 4,
        out_specs=(vmem,) * 5,
        scratch_shapes=[
            pltpu.SMEM(owner_counts.shape, jnp.int32),
            pltpu.VMEM((1, tiles), jnp.int32),
            pltpu.VMEM((orbitals, electrons), BF),
            pltpu.VMEM((orbitals, electrons), BF),
            wide_scratch,
            pltpu.SemaphoreType.DMA((4,)),
        ],
        compiler_params=params,
        name="green",
    )(*(in_place(x) for x in (owner_counts, pattern_row, green_factor[0], trial)))
    arrived = lax.all_to_all(
        outgoing.reshape(devices, half, entries), both, split_axis=0, concat_axis=0
    )
    partial_bias, held = pl.pallas_call(
        functools.partial(bias_kernel, walkers=devices, half=half, block=block),
        out_shape=(
            jax.ShapeDtypeStruct((devices * lanes, LANES), BF),
            jax.ShapeDtypeStruct((half, vectors, entries), BF),
        ),
        in_specs=[vmem, hbm],
        out_specs=(vmem,) * 2,
        scratch_shapes=[
            pltpu.VMEM((entries // LANES, half * devices, LANES), F32),
            pltpu.VMEM((devices, half * entries), BF),
            pltpu.VMEM((devices * lanes, LANES), F32),
            pltpu.SemaphoreType.DMA((vectors // block,)),
        ],
        compiler_params=streaming,
        cost_estimate=pl.CostEstimate(
            flops=flops, transcendentals=0, bytes_accessed=tile_bytes
        ),
        name="bias",
    )(arrived.reshape(devices * half, entries), chol)
    partial_bias = lax.all_to_all(
        partial_bias.reshape(devices, lanes, LANES), both, split_axis=0, concat_axis=0
    )
    fields, summand = pl.pallas_call(
        functools.partial(field_kernel, devices=devices),
        out_shape=(
            jax.ShapeDtypeStruct((devices, lanes, LANES), BF),
            jax.ShapeDtypeStruct((lanes, LANES), F32),
        ),
        in_specs=[vmem] * 4,
        out_specs=(vmem,) * 2,
        compiler_params=params,
        name="fields",
    )(partial_bias, aux, chol_group.reshape(lanes, LANES), group_weight.reshape(1, -1))
    fields = lax.all_to_all(fields, both, split_axis=0, concat_axis=0)
    potential = pl.pallas_call(
        functools.partial(potential_kernel, walkers=devices, half=half),
        out_shape=jax.ShapeDtypeStruct((devices * half, entries), BF),
        in_specs=[vmem, vmem],
        out_specs=vmem,
        scratch_shapes=[
            pltpu.VMEM((devices * lanes, LANES), F32),
            pltpu.VMEM((devices, vectors), BF),
            pltpu.VMEM((entries // LANES, half * devices, LANES), F32),
        ],
        compiler_params=streaming,
        cost_estimate=pl.CostEstimate(
            flops=flops, transcendentals=0, bytes_accessed=tile_bytes
        ),
        name="potential",
    )(fields.reshape(devices * lanes, LANES), held)
    returned = lax.all_to_all(
        potential.reshape(devices, half, entries), both, split_axis=0, concat_axis=0
    )
    advanced, log_weight = pl.pallas_call(
        functools.partial(advance_kernel, side=side),
        out_shape=(
            jax.ShapeDtypeStruct((orbitals, electrons), BF),
            jax.ShapeDtypeStruct((1,), F32),
        ),
        in_specs=[vmem] * 7,
        out_specs=(vmem, smem),
        scratch_shapes=[wide_scratch],
        compiler_params=params,
        name="advance",
    )(returned.reshape(devices * half, entries), *choices, walkers[0], summand)
    return advanced[None], log_weight


def solution(mesh):
    return jax.shard_map(
        functools.partial(
            per_device, groups=mesh.shape["groups"], owners=mesh.shape["tile"]
        ),
        mesh=mesh,
        in_specs=(
            P(("groups", "tile"), None, None),
            P(("groups", "tile"), None, None),
            P(),
            P("tile", None, None),
            P(),
            P(),
            P(),
            P(),
            P("groups", None),
        ),
        out_specs=(P(("groups", "tile"), None, None), P(("groups", "tile"))),
        check_vma=False,
    )
```

```python
import functools
import math

import jax
import jax.numpy as jnp
from jax import lax
from jax.experimental import pallas as pl
from jax.experimental.pallas import tpu as pltpu
from jax.sharding import PartitionSpec as P

BF = jnp.bfloat16
F32 = jnp.float32
LANES = 128
VMEM_LIMIT = 8 * 1024 * 1024


def log2(n):
    bits = n.bit_length() - 1
    assert 1 << bits == n
    return bits


def iota(shape, axis):
    return lax.broadcasted_iota(jnp.int32, shape, axis)


def one_hot(equal):
    return jnp.where(equal, 1.0, 0.0).astype(BF)


def mm(a, b):
    return jnp.dot(a, b, preferred_element_type=F32)


def nt(a, b):
    return lax.dot_general(a, b, (((1,), (1,)), ((), ())), preferred_element_type=F32)


def tn(a, b):
    return lax.dot_general(a, b, (((0,), (0,)), ((), ())), preferred_element_type=F32)


def slot_of_tile(counts_ref, tiles, owners, groups, half, cap):
    tile = iota((1, tiles), 1)
    owner = jnp.zeros((1, tiles), jnp.int32)
    first = jnp.zeros((1, tiles), jnp.int32)
    offset = jnp.int32(0)
    for d in range(owners):
        offset = offset + counts_ref[d]
        past = tile >= offset
        owner = jnp.where(past, d + 1, owner)
        first = jnp.where(past, offset, first)
    place = tile - first
    slot = owner * half + place
    for x in range(1, groups):
        start = min(x * half, cap - half)
        slot = jnp.where(place >= x * half, (x * owners + owner) * half + place - start, slot)
    return slot


def row_of(pat, nblk, side):
    row_block = pat >> log2(nblk)
    col_block = pat & (nblk - 1)
    per = LANES // side
    return ((col_block >> log2(per)) << log2(nblk)) + row_block, col_block & (per - 1)


def tile_columns(pattern_ref, tiles, nblk, side):
    pat = jnp.broadcast_to(pattern_ref[...].astype(F32), (LANES, tiles)).T.astype(jnp.int32)
    return row_of(pat, nblk, side)


def green_kernel(
    counts_hbm, pattern_hbm, factor_hbm, trial_hbm, chol_ref,
    out_ref, fold_ref, slot_ref, pick_ref, inside_ref, early_ref,
    counts_ref, pattern_ref, factor_ref, trial_ref, wide_ref, sems,
    *, owners, groups, half, cap, side,
):
    copies = [
        pltpu.make_async_copy(source, held, sems.at[i])
        for i, (source, held) in enumerate(
            [
                (counts_hbm, counts_ref),
                (pattern_hbm, pattern_ref),
                (factor_hbm, factor_ref),
                (trial_hbm, trial_ref),
            ]
        )
    ]
    for copy in copies:
        copy.start()
    orbitals = factor_ref.shape[0]
    nblk = orbitals // side
    tiles = pattern_ref.shape[1]
    slots = out_ref.shape[0]
    wide = orbitals // LANES
    assert wide * nblk == LANES
    src = iota(fold_ref.shape, 0)
    dst = iota(fold_ref.shape, 1)
    fold_ref[...] = one_hot(((src >> log2(LANES)) << log2(side)) + (src & (side - 1)) == dst)
    copies[0].wait()
    copies[1].wait()
    where_row, place = tile_columns(pattern_ref, tiles, nblk, side)
    lane = iota((tiles, LANES), 1)
    pick = one_hot(where_row == lane)
    inside = place == (lane >> log2(side))
    pick_ref[...] = pick
    inside_ref[...] = jnp.where(inside, 1.0, 0.0)
    slot = slot_of_tile(counts_ref, tiles, owners, groups, half, cap)
    slot_ref[...] = one_hot(iota((slots, tiles), 0) == slot)
    copies[2].wait()
    copies[3].wait()
    early = pltpu.make_async_copy(
        chol_ref.at[pl.ds(first_slot(half, cap), half), pl.ds(0, early_ref.shape[1]), :],
        early_ref,
        sems.at[4],
    )
    early.start()
    green = nt(factor_ref[...], trial_ref[...])
    for k in range(wide):
        wide_ref[k] = green[:, k * LANES : (k + 1) * LANES]
    values = jnp.zeros((tiles, side * side), F32)
    count = 2
    for g in range(side // count):
        cut = jnp.concatenate(
            [
                jnp.concatenate(
                    [
                        wide_ref[k, pl.ds(g * count + p, nblk, stride=side), :]
                        for p in range(count)
                    ],
                    axis=1,
                ).astype(BF)
                for k in range(wide)
            ],
            axis=0,
        )
        found = mm(pick, cut)
        kept = jnp.concatenate(
            [
                jnp.where(inside, found[:, p * LANES : (p + 1) * LANES], 0.0).astype(BF)
                for p in range(count)
            ],
            axis=1,
        )
        span = count * LANES
        values = values + mm(kept, fold_ref[g * span : (g + 1) * span, :])
    values = values.astype(BF)
    out_ref[...] = mm(slot_ref[...], values).astype(BF)
    early.wait()


def in_place(x):
    return pltpu.with_memory_space_constraint(x, pltpu.HBM)


def first_slot(half, cap):
    return jnp.minimum(lax.axis_index("groups") * half, cap - half)


def bias_kernel(
    green_ref, early_ref, chol_ref, out_ref, held, tall, left, back, sems,
    *, walkers, half, block,
):
    entries = green_ref.shape[1]
    ready = early_ref.shape[1]
    lanes = (ready + held.shape[1]) // LANES
    narrow = entries // LANES
    steps = held.shape[1] // block
    first = first_slot(half, chol_ref.shape[0])

    def fetch(s):
        rows = pl.ds(s * block if isinstance(s, int) else pl.multiple_of(s * block, block), block)
        start = ready + s * block
        source = pl.ds(start if isinstance(s, int) else pl.multiple_of(start, block), block)
        return pltpu.make_async_copy(
            chol_ref.at[pl.ds(first, half), source, :], held.at[:, rows, :], sems.at[s]
        )

    for s in range(steps):
        fetch(s).start()
    for k in range(narrow):
        tall[k] = green_ref[:, k * LANES : (k + 1) * LANES].astype(F32)
    for j in range(half):
        for k in range(narrow):
            at = j * entries + k * LANES
            left[:, at : at + LANES] = tall[k, pl.ds(j, walkers, stride=half), :].astype(BF)

    def product(source, s, base):
        rows = pl.ds(pl.multiple_of(s * block, block), block)
        right = jnp.concatenate([source[j, rows, :] for j in range(half)], axis=1)
        total = nt(left[...], right)
        for i in range(block // LANES):
            place = base + s * (block // LANES) + i
            back[pl.ds(place, walkers, stride=lanes), :] = total[:, i * LANES : (i + 1) * LANES]

    def first_step(s, carry):
        product(early_ref, s, 0)
        return carry

    def step(s, carry):
        fetch(s).wait()
        product(held, s, ready // LANES)
        return carry

    lax.fori_loop(0, ready // block, first_step, 0)
    lax.fori_loop(0, steps, step, 0)
    out_ref[...] = back[...].astype(BF)


def field_kernel(partial_ref, aux_ref, group_ref, weight_ref, fields_ref, summand_ref, *, devices):
    lanes = group_ref.shape[0]
    bias = partial_ref[0].astype(F32)
    for i in range(1, devices):
        bias = bias + partial_ref[i].astype(F32)
    draws = aux_ref[pl.ds(lax.axis_index("tile"), 1), :]
    draws = jnp.concatenate(
        [draws[:, i * LANES : (i + 1) * LANES] for i in range(lanes)], axis=0
    )
    sampled = draws.astype(F32) * (1.0 / 262144.0)
    scale = jnp.zeros((lanes, LANES), F32)
    for k in range(weight_ref.shape[1]):
        scale = jnp.where(group_ref[...] == k, weight_ref[:, k : k + 1], scale)
    fields = (scale * (sampled - bias)).astype(BF)
    for i in range(devices):
        fields_ref[i] = fields
    summand_ref[...] = sampled * bias - 0.5 * bias * bias


def potential_kernel(
    fields_ref, early_ref, held, out_ref, tall, left, back, *, walkers, half
):
    ready = early_ref.shape[1]
    entries = held.shape[2]
    lanes = left.shape[1] // LANES
    narrow = entries // LANES
    tall[...] = fields_ref[...].astype(F32)
    for i in range(lanes):
        left[:, i * LANES : (i + 1) * LANES] = tall[pl.ds(i, walkers, stride=lanes), :].astype(BF)
    count = 4 if half % 4 == 0 else 1

    def step(s, carry):
        for i in range(count):
            j = s * count + i
            tile = mm(left[:, :ready], early_ref[j]) + mm(left[:, ready:], held[j])
            for k in range(narrow):
                back[k, pl.ds(j, walkers, stride=half), :] = tile[:, k * LANES : (k + 1) * LANES]
        return carry

    lax.fori_loop(0, half // count, step, 0)
    for k in range(narrow):
        out_ref[:, k * LANES : (k + 1) * LANES] = back[k].astype(BF)


def advance_kernel(
    tiles_ref, fold_ref, slot_ref, pick_ref, inside_ref, walker_ref, summand_ref,
    out_ref, logw_ref, wide_ref, *, side,
):
    logw_ref[0] = jnp.sum(summand_ref[...])
    orbitals = walker_ref.shape[0]
    nblk = orbitals // side
    wide = orbitals // LANES
    values = tn(slot_ref[...], tiles_ref[...]).astype(BF)
    repeated = nt(values, fold_ref[...])
    inside = inside_ref[...]
    kept = jnp.concatenate(
        [(repeated[:, p * LANES : (p + 1) * LANES] * inside).astype(BF) for p in range(side)],
        axis=1,
    )
    cut = tn(pick_ref[...], kept)
    for k in range(wide):
        for p in range(side):
            wide_ref[k, pl.ds(p, nblk, stride=side), :] = cut[
                k * nblk : (k + 1) * nblk, p * LANES : (p + 1) * LANES
            ]
    potential = jnp.concatenate([wide_ref[k].astype(BF) for k in range(wide)], axis=1)
    terms = [walker_ref[...]]
    rows = orbitals // 2
    for degree in range(1, 5):
        term = [
            (mm(potential[i * rows : (i + 1) * rows], terms[-1]) / degree).astype(BF)
            for i in range(2)
        ]
        terms.append(jnp.concatenate(term, axis=0))
    running = terms[0].astype(F32)
    for term in terms[1:]:
        running = running + term.astype(F32)
    out_ref[...] = running.astype(BF)


def per_device(
    walkers, green_factor, trial, chol, pattern, owner_counts, chol_group, group_weight, aux, *, groups, owners
):
    devices = groups * owners
    walk_dev, orbitals, electrons = walkers.shape
    assert walk_dev == 1
    cap, vectors, entries = chol.shape
    side = math.isqrt(entries)
    lanes = vectors // LANES
    half = -(-cap // groups)
    tiles = pattern.shape[0]
    both = ("groups", "tile")
    pattern_row = pattern.reshape(1, tiles)

    smem = pl.BlockSpec(memory_space=pltpu.SMEM)
    vmem = pl.BlockSpec(memory_space=pltpu.VMEM)
    params = pltpu.CompilerParams(vmem_limit_bytes=VMEM_LIMIT)
    in_hbm = pl.BlockSpec(memory_space=pltpu.HBM)
    streaming = pltpu.CompilerParams(
        vmem_limit_bytes=VMEM_LIMIT + 2 * half * vectors * entries
    )
    sizes = dict(owners=owners, groups=groups, half=half, cap=cap, side=side)
    block = min(256, vectors // 2)
    ready = block
    tile_bytes = half * vectors * entries * 2
    flops = 2 * devices * half * vectors * entries
    wide_scratch = pltpu.VMEM((orbitals // LANES, orbitals, LANES), F32)

    outgoing, *choices, early = pl.pallas_call(
        functools.partial(green_kernel, **sizes),
        out_shape=(
            jax.ShapeDtypeStruct((devices * half, entries), BF),
            jax.ShapeDtypeStruct((side * LANES, entries), BF),
            jax.ShapeDtypeStruct((devices * half, tiles), BF),
            jax.ShapeDtypeStruct((tiles, LANES), BF),
            jax.ShapeDtypeStruct((tiles, LANES), F32),
            jax.ShapeDtypeStruct((half, ready, entries), BF),
        ),
        in_specs=[in_hbm] * 5,
        out_specs=(vmem,) * 6,
        scratch_shapes=[
            pltpu.SMEM(owner_counts.shape, jnp.int32),
            pltpu.VMEM((1, tiles), jnp.int32),
            pltpu.VMEM((orbitals, electrons), BF),
            pltpu.VMEM((orbitals, electrons), BF),
            wide_scratch,
            pltpu.SemaphoreType.DMA((5,)),
        ],
        compiler_params=params,
        name="green",
    )(*(in_place(x) for x in (owner_counts, pattern_row, green_factor[0], trial)), in_place(chol))
    arrived = lax.all_to_all(
        outgoing.reshape(devices, half, entries), both, split_axis=0, concat_axis=0
    )
    partial_bias, held = pl.pallas_call(
        functools.partial(bias_kernel, walkers=devices, half=half, block=block),
        out_shape=(
            jax.ShapeDtypeStruct((devices * lanes, LANES), BF),
            jax.ShapeDtypeStruct((half, vectors - ready, entries), BF),
        ),
        in_specs=[vmem, vmem, in_hbm],
        out_specs=(vmem,) * 2,
        scratch_shapes=[
            pltpu.VMEM((entries // LANES, half * devices, LANES), F32),
            pltpu.VMEM((devices, half * entries), BF),
            pltpu.VMEM((devices * lanes, LANES), F32),
            pltpu.SemaphoreType.DMA(((vectors - ready) // block,)),
        ],
        compiler_params=streaming,
        cost_estimate=pl.CostEstimate(
            flops=flops, transcendentals=0, bytes_accessed=tile_bytes
        ),
        name="bias",
    )(arrived.reshape(devices * half, entries), early, in_place(chol))
    partial_bias = lax.all_to_all(
        partial_bias.reshape(devices, lanes, LANES), both, split_axis=0, concat_axis=0
    )
    fields, summand = pl.pallas_call(
        functools.partial(field_kernel, devices=devices),
        out_shape=(
            jax.ShapeDtypeStruct((devices, lanes, LANES), BF),
            jax.ShapeDtypeStruct((lanes, LANES), F32),
        ),
        in_specs=[vmem] * 4,
        out_specs=(vmem,) * 2,
        compiler_params=params,
        name="fields",
    )(partial_bias, aux, chol_group.reshape(lanes, LANES), group_weight.reshape(1, -1))
    fields = lax.all_to_all(fields, both, split_axis=0, concat_axis=0)
    potential = pl.pallas_call(
        functools.partial(potential_kernel, walkers=devices, half=half),
        out_shape=jax.ShapeDtypeStruct((devices * half, entries), BF),
        in_specs=[vmem] * 3,
        out_specs=vmem,
        scratch_shapes=[
            pltpu.VMEM((devices * lanes, LANES), F32),
            pltpu.VMEM((devices, vectors), BF),
            pltpu.VMEM((entries // LANES, half * devices, LANES), F32),
        ],
        compiler_params=streaming,
        cost_estimate=pl.CostEstimate(
            flops=flops, transcendentals=0, bytes_accessed=tile_bytes
        ),
        name="potential",
    )(fields.reshape(devices * lanes, LANES), early, held)
    returned = lax.all_to_all(
        potential.reshape(devices, half, entries), both, split_axis=0, concat_axis=0
    )
    advanced, log_weight = pl.pallas_call(
        functools.partial(advance_kernel, side=side),
        out_shape=(
            jax.ShapeDtypeStruct((orbitals, electrons), BF),
            jax.ShapeDtypeStruct((1,), F32),
        ),
        in_specs=[vmem] * 7,
        out_specs=(vmem, smem),
        scratch_shapes=[wide_scratch],
        compiler_params=params,
        name="advance",
    )(returned.reshape(devices * half, entries), *choices, walkers[0], summand)
    return advanced[None], log_weight


def solution(mesh):
    return jax.shard_map(
        functools.partial(
            per_device, groups=mesh.shape["groups"], owners=mesh.shape["tile"]
        ),
        mesh=mesh,
        in_specs=(
            P(("groups", "tile"), None, None),
            P(("groups", "tile"), None, None),
            P(),
            P("tile", None, None),
            P(),
            P(),
            P(),
            P(),
            P("groups", None),
        ),
        out_specs=(P(("groups", "tile"), None, None), P(("groups", "tile"))),
        check_vma=False,
    )
```

```python
import functools
import math

import jax
import jax.numpy as jnp
from jax import lax
from jax.experimental import pallas as pl
from jax.experimental.pallas import tpu as pltpu
from jax.sharding import PartitionSpec as P

BF = jnp.bfloat16
F32 = jnp.float32
LANES = 128
VMEM_LIMIT = 8 * 1024 * 1024


def log2(n):
    bits = n.bit_length() - 1
    assert 1 << bits == n
    return bits


def iota(shape, axis):
    return lax.broadcasted_iota(jnp.int32, shape, axis)


def one_hot(equal):
    return jnp.where(equal, 1.0, 0.0).astype(BF)


def mm(a, b):
    return jnp.dot(a, b, preferred_element_type=F32)


def nt(a, b):
    return lax.dot_general(a, b, (((1,), (1,)), ((), ())), preferred_element_type=F32)


def tn(a, b):
    return lax.dot_general(a, b, (((0,), (0,)), ((), ())), preferred_element_type=F32)


def slot_of_tile(counts_ref, tiles, owners, groups, half, cap):
    tile = iota((1, tiles), 1)
    owner = jnp.zeros((1, tiles), jnp.int32)
    first = jnp.zeros((1, tiles), jnp.int32)
    offset = jnp.int32(0)
    for d in range(owners):
        offset = offset + counts_ref[d]
        past = tile >= offset
        owner = jnp.where(past, d + 1, owner)
        first = jnp.where(past, offset, first)
    place = tile - first
    slot = owner * half + place
    for x in range(1, groups):
        start = min(x * half, cap - half)
        slot = jnp.where(place >= x * half, (x * owners + owner) * half + place - start, slot)
    return slot


def row_of(pat, nblk, side):
    row_block = pat >> log2(nblk)
    col_block = pat & (nblk - 1)
    per = LANES // side
    return ((col_block >> log2(per)) << log2(nblk)) + row_block, col_block & (per - 1)


def tile_columns(pattern_ref, tiles, nblk, side):
    pat = jnp.broadcast_to(pattern_ref[...].astype(F32), (LANES, tiles)).T.astype(jnp.int32)
    return row_of(pat, nblk, side)


def green_kernel(
    counts_hbm, pattern_hbm, factor_hbm, trial_hbm,
    out_ref, fold_ref, slot_ref, pick_ref, inside_ref,
    counts_ref, pattern_ref, factor_ref, trial_ref, wide_ref, sems,
    *, owners, groups, half, cap, side,
):
    copies = [
        pltpu.make_async_copy(source, held, sems.at[i])
        for i, (source, held) in enumerate(
            [
                (counts_hbm, counts_ref),
                (pattern_hbm, pattern_ref),
                (factor_hbm, factor_ref),
                (trial_hbm, trial_ref),
            ]
        )
    ]
    for copy in copies:
        copy.start()
    orbitals = factor_ref.shape[0]
    nblk = orbitals // side
    tiles = pattern_ref.shape[1]
    slots = out_ref.shape[0]
    wide = orbitals // LANES
    assert wide * nblk == LANES
    src = iota(fold_ref.shape, 0)
    dst = iota(fold_ref.shape, 1)
    fold_ref[...] = one_hot(((src >> log2(LANES)) << log2(side)) + (src & (side - 1)) == dst)
    copies[0].wait()
    copies[1].wait()
    where_row, place = tile_columns(pattern_ref, tiles, nblk, side)
    lane = iota((tiles, LANES), 1)
    pick = one_hot(where_row == lane)
    inside = place == (lane >> log2(side))
    pick_ref[...] = pick
    inside_ref[...] = jnp.where(inside, 1.0, 0.0)
    slot = slot_of_tile(counts_ref, tiles, owners, groups, half, cap)
    slot_ref[...] = one_hot(iota((slots, tiles), 0) == slot)
    copies[2].wait()
    copies[3].wait()
    green = nt(factor_ref[...], trial_ref[...])
    for k in range(wide):
        wide_ref[k] = green[:, k * LANES : (k + 1) * LANES]
    values = jnp.zeros((tiles, side * side), F32)
    count = 2
    for g in range(side // count):
        cut = jnp.concatenate(
            [
                jnp.concatenate(
                    [
                        wide_ref[k, pl.ds(g * count + p, nblk, stride=side), :]
                        for p in range(count)
                    ],
                    axis=1,
                ).astype(BF)
                for k in range(wide)
            ],
            axis=0,
        )
        found = mm(pick, cut)
        kept = jnp.concatenate(
            [
                jnp.where(inside, found[:, p * LANES : (p + 1) * LANES], 0.0).astype(BF)
                for p in range(count)
            ],
            axis=1,
        )
        span = count * LANES
        values = values + mm(kept, fold_ref[g * span : (g + 1) * span, :])
    values = values.astype(BF)
    out_ref[...] = mm(slot_ref[...], values).astype(BF)


def in_place(x):
    return pltpu.with_memory_space_constraint(x, pltpu.HBM)


def first_slot(half, cap):
    return jnp.minimum(lax.axis_index("groups") * half, cap - half)


def bias_kernel(
    green_ref, chol_ref, out_ref, held, tall, left, back, sems, *, walkers, half, block
):
    entries = green_ref.shape[1]
    vectors = held.shape[1]
    lanes = vectors // LANES
    narrow = entries // LANES
    steps = vectors // block
    first = first_slot(half, chol_ref.shape[0])

    def fetch(s):
        rows = pl.ds(s * block if isinstance(s, int) else pl.multiple_of(s * block, block), block)
        return pltpu.make_async_copy(
            chol_ref.at[pl.ds(first, half), rows, :], held.at[:, rows, :], sems.at[s]
        )

    for s in range(steps):
        fetch(s).start()
    for k in range(narrow):
        tall[k] = green_ref[:, k * LANES : (k + 1) * LANES].astype(F32)
    for j in range(half):
        for k in range(narrow):
            at = j * entries + k * LANES
            left[:, at : at + LANES] = tall[k, pl.ds(j, walkers, stride=half), :].astype(BF)

    def step(s, carry):
        fetch(s).wait()
        rows = pl.ds(pl.multiple_of(s * block, block), block)
        right = jnp.concatenate([held[j, rows, :] for j in range(half)], axis=1)
        total = nt(left[...], right)
        for i in range(block // LANES):
            place = s * (block // LANES) + i
            back[pl.ds(place, walkers, stride=lanes), :] = total[:, i * LANES : (i + 1) * LANES]
        return carry

    lax.fori_loop(0, steps, step, 0)
    out_ref[...] = back[...].astype(BF)


def field_kernel(partial_ref, aux_ref, group_ref, weight_ref, fields_ref, summand_ref, *, devices):
    lanes = group_ref.shape[0]
    bias = partial_ref[0].astype(F32)
    for i in range(1, devices):
        bias = bias + partial_ref[i].astype(F32)
    draws = aux_ref[pl.ds(lax.axis_index("tile"), 1), :]
    draws = jnp.concatenate(
        [draws[:, i * LANES : (i + 1) * LANES] for i in range(lanes)], axis=0
    )
    sampled = draws.astype(F32) * (1.0 / 262144.0)
    scale = jnp.zeros((lanes, LANES), F32)
    for k in range(weight_ref.shape[1]):
        scale = jnp.where(group_ref[...] == k, weight_ref[:, k : k + 1], scale)
    fields = (scale * (sampled - bias)).astype(BF)
    for i in range(devices):
        fields_ref[i] = fields
    summand_ref[...] = sampled * bias - 0.5 * bias * bias


def potential_kernel(fields_ref, held, out_ref, tall, left, back, *, walkers, half):
    entries = held.shape[2]
    lanes = left.shape[1] // LANES
    narrow = entries // LANES
    tall[...] = fields_ref[...].astype(F32)
    for i in range(lanes):
        left[:, i * LANES : (i + 1) * LANES] = tall[pl.ds(i, walkers, stride=lanes), :].astype(BF)
    count = 8 if half % 8 == 0 else 1

    def step(s, carry):
        for i in range(count):
            j = s * count + i
            tile = mm(left[...], held[j])
            for k in range(narrow):
                back[k, pl.ds(j, walkers, stride=half), :] = tile[:, k * LANES : (k + 1) * LANES]
        return carry

    lax.fori_loop(0, half // count, step, 0)
    for k in range(narrow):
        out_ref[:, k * LANES : (k + 1) * LANES] = back[k].astype(BF)


def advance_kernel(
    tiles_ref, fold_ref, slot_ref, pick_ref, inside_ref, walker_ref, summand_ref,
    out_ref, logw_ref, wide_ref, *, side,
):
    logw_ref[0] = jnp.sum(summand_ref[...])
    orbitals = walker_ref.shape[0]
    nblk = orbitals // side
    wide = orbitals // LANES
    values = tn(slot_ref[...], tiles_ref[...]).astype(BF)
    repeated = nt(values, fold_ref[...])
    inside = inside_ref[...]
    kept = jnp.concatenate(
        [(repeated[:, p * LANES : (p + 1) * LANES] * inside).astype(BF) for p in range(side)],
        axis=1,
    )
    cut = tn(pick_ref[...], kept)
    for k in range(wide):
        for p in range(side):
            wide_ref[k, pl.ds(p, nblk, stride=side), :] = cut[
                k * nblk : (k + 1) * nblk, p * LANES : (p + 1) * LANES
            ]
    potential = jnp.concatenate([wide_ref[k].astype(BF) for k in range(wide)], axis=1)
    terms = [walker_ref[...]]
    rows = orbitals // 2
    for degree in range(1, 5):
        term = [
            (mm(potential[i * rows : (i + 1) * rows], terms[-1]) / degree).astype(BF)
            for i in range(2)
        ]
        terms.append(jnp.concatenate(term, axis=0))
    running = terms[0].astype(F32)
    for term in terms[1:]:
        running = running + term.astype(F32)
    out_ref[...] = running.astype(BF)


def per_device(
    walkers, green_factor, trial, chol, pattern, owner_counts, chol_group, group_weight, aux, *, groups, owners
):
    devices = groups * owners
    walk_dev, orbitals, electrons = walkers.shape
    assert walk_dev == 1
    cap, vectors, entries = chol.shape
    side = math.isqrt(entries)
    lanes = vectors // LANES
    half = -(-cap // groups)
    tiles = pattern.shape[0]
    both = ("groups", "tile")
    pattern_row = pattern.reshape(1, tiles)

    smem = pl.BlockSpec(memory_space=pltpu.SMEM)
    vmem = pl.BlockSpec(memory_space=pltpu.VMEM)
    params = pltpu.CompilerParams(vmem_limit_bytes=VMEM_LIMIT)
    hbm = pl.BlockSpec(memory_space=pl.ANY)
    in_hbm = pl.BlockSpec(memory_space=pltpu.HBM)
    streaming = pltpu.CompilerParams(
        vmem_limit_bytes=VMEM_LIMIT + 2 * half * vectors * entries
    )
    sizes = dict(owners=owners, groups=groups, half=half, cap=cap, side=side)
    block = min(256, vectors)
    tile_bytes = half * vectors * entries * 2
    flops = 2 * devices * half * vectors * entries
    wide_scratch = pltpu.VMEM((orbitals // LANES, orbitals, LANES), F32)

    outgoing, *choices = pl.pallas_call(
        functools.partial(green_kernel, **sizes),
        out_shape=(
            jax.ShapeDtypeStruct((devices * half, entries), BF),
            jax.ShapeDtypeStruct((side * LANES, entries), BF),
            jax.ShapeDtypeStruct((devices * half, tiles), BF),
            jax.ShapeDtypeStruct((tiles, LANES), BF),
            jax.ShapeDtypeStruct((tiles, LANES), F32),
        ),
        in_specs=[in_hbm] * 4,
        out_specs=(vmem,) * 5,
        scratch_shapes=[
            pltpu.SMEM(owner_counts.shape, jnp.int32),
            pltpu.VMEM((1, tiles), jnp.int32),
            pltpu.VMEM((orbitals, electrons), BF),
            pltpu.VMEM((orbitals, electrons), BF),
            wide_scratch,
            pltpu.SemaphoreType.DMA((4,)),
        ],
        compiler_params=params,
        name="green",
    )(*(in_place(x) for x in (owner_counts, pattern_row, green_factor[0], trial)))
    arrived = lax.all_to_all(
        outgoing.reshape(devices, half, entries), both, split_axis=0, concat_axis=0
    )
    partial_bias, held = pl.pallas_call(
        functools.partial(bias_kernel, walkers=devices, half=half, block=block),
        out_shape=(
            jax.ShapeDtypeStruct((devices * lanes, LANES), BF),
            jax.ShapeDtypeStruct((half, vectors, entries), BF),
        ),
        in_specs=[vmem, hbm],
        out_specs=(vmem,) * 2,
        scratch_shapes=[
            pltpu.VMEM((entries // LANES, half * devices, LANES), F32),
            pltpu.VMEM((devices, half * entries), BF),
            pltpu.VMEM((devices * lanes, LANES), F32),
            pltpu.SemaphoreType.DMA((vectors // block,)),
        ],
        compiler_params=streaming,
        cost_estimate=pl.CostEstimate(
            flops=flops, transcendentals=0, bytes_accessed=tile_bytes
        ),
        name="bias",
    )(arrived.reshape(devices * half, entries), chol)
    partial_bias = lax.all_to_all(
        partial_bias.reshape(devices, lanes, LANES), both, split_axis=0, concat_axis=0
    )
    fields, summand = pl.pallas_call(
        functools.partial(field_kernel, devices=devices),
        out_shape=(
            jax.ShapeDtypeStruct((devices, lanes, LANES), BF),
            jax.ShapeDtypeStruct((lanes, LANES), F32),
        ),
        in_specs=[vmem] * 4,
        out_specs=(vmem,) * 2,
        compiler_params=params,
        name="fields",
    )(partial_bias, aux, chol_group.reshape(lanes, LANES), group_weight.reshape(1, -1))
    fields = lax.all_to_all(fields, both, split_axis=0, concat_axis=0)
    potential = pl.pallas_call(
        functools.partial(potential_kernel, walkers=devices, half=half),
        out_shape=jax.ShapeDtypeStruct((devices * half, entries), BF),
        in_specs=[vmem, vmem],
        out_specs=vmem,
        scratch_shapes=[
            pltpu.VMEM((devices * lanes, LANES), F32),
            pltpu.VMEM((devices, vectors), BF),
            pltpu.VMEM((entries // LANES, half * devices, LANES), F32),
        ],
        compiler_params=streaming,
        cost_estimate=pl.CostEstimate(
            flops=flops, transcendentals=0, bytes_accessed=tile_bytes
        ),
        name="potential",
    )(fields.reshape(devices * lanes, LANES), held)
    returned = lax.all_to_all(
        potential.reshape(devices, half, entries), both, split_axis=0, concat_axis=0
    )
    advanced, log_weight = pl.pallas_call(
        functools.partial(advance_kernel, side=side),
        out_shape=(
            jax.ShapeDtypeStruct((orbitals, electrons), BF),
            jax.ShapeDtypeStruct((1,), F32),
        ),
        in_specs=[vmem] * 7,
        out_specs=(vmem, smem),
        scratch_shapes=[wide_scratch],
        compiler_params=params,
        name="advance",
    )(returned.reshape(devices * half, entries), *choices, walkers[0], summand)
    return advanced[None], log_weight


def solution(mesh):
    return jax.shard_map(
        functools.partial(
            per_device, groups=mesh.shape["groups"], owners=mesh.shape["tile"]
        ),
        mesh=mesh,
        in_specs=(
            P(("groups", "tile"), None, None),
            P(("groups", "tile"), None, None),
            P(),
            P("tile", None, None),
            P(),
            P(),
            P(),
            P(),
            P("groups", None),
        ),
        out_specs=(P(("groups", "tile"), None, None), P(("groups", "tile"))),
        check_vma=False,
    )
```
